32 devices in a mesh: pipe: 4 (over z), tensor: 4 (over y, core), seq: 2 (over x).
Axes of the slice: x: 2, y: 2, z: 4, core: 2. Of those that a mesh axis runs over, the one named last changes fastest.
Arguments:
- tokens: bfloat16 [384, 4096], P('seq', 'tensor'), parts along dimension 0
- norm_gain: bfloat16 [4, 4096], P('pipe', 'tensor'), may hold values from 0.25 to 1.75
- query_weight: bfloat16 [4, 4096, 2048], P('pipe', None, 'tensor')
- kv_weight: bfloat16 [4, 4096, 1024], P('pipe', None, 'tensor')
- out_weight: bfloat16 [4, 2048, 4096], P('pipe', None, 'tensor'), may hold values from -0.25 to 0.25
- window_blocks: int32 [24, 4], P('seq'), parts along dimension 0, may hold values from 0 to 12, as said below
Outputs:
- section_states: bfloat16 [4, 384, 4096], P('pipe', 'seq', 'tensor'), parts along dimension 1
The draws below stay inside these ranges and needn't reach their ends.
There are 2 independent parts, one for each index of `seq`. The reference program is written for one: setup_inputs(seed, part) draws one part's arguments, and reference() takes and returns one part's arrays. A program takes and returns all parts, laid end to end along the dimension named above; an argument that names none is the same for every part. Nothing has to cross between parts.
Inputs may be any that keep to these rules, and one draw needn't show every extreme that they name: `window_blocks`: row b lists the key blocks that query block b sees: b itself, then b - 1, then two distinct blocks below b - 1; a slot without such a block holds 12.
All inputs are finite; a program needn't handle non-finite values.
Results may differ from the reference program's by a relative error of at most 0.0095.
Values may be sent and summed in bfloat16 or wider, within the bound.
A program may use at most 64 MiB of HBM per device.

```python
import math
import jax
import jax.numpy as jnp
from jax import lax

D = 4096
HD = 128
HQ = 16
KVH = 4
BLK = 16
SECTIONS = 4
TOK = 192
NBLK = 12


def normal_part(key, label, shape):
    return jax.random.normal(jax.random.fold_in(key, label), shape, jnp.float32)


def draw_kv_weight(key, part):
    keys = normal_part(key, 7, (SECTIONS, D, KVH * HD))
    values = normal_part(key, 8, (SECTIONS, D, KVH * HD))
    return (jnp.concatenate([keys, values], axis=2) / math.sqrt(D)).astype(jnp.bfloat16)


def draw_query_weight(key, part):
    base = normal_part(key, 9, (SECTIONS, D, HQ * HD)) / math.sqrt(D)
    return base.astype(jnp.bfloat16)


def draw_tokens(key, part):
    base = normal_part(key, 3, (TOK, D))
    columns = jnp.exp(jax.random.uniform(jax.random.fold_in(key, 4), (1, D), jnp.float32, math.log(0.3), math.log(3.0)))
    return (base * columns).astype(jnp.bfloat16)


def draw_window_blocks(key, part):
    row_ids = jnp.arange(NBLK, dtype=jnp.int32)[:, None]
    col_ids = jnp.arange(NBLK, dtype=jnp.int32)[None, :]
    scores = jax.random.randint(key, (NBLK, NBLK), 0, 4096, jnp.int32) * NBLK + col_ids
    scores = jnp.where(col_ids <= row_ids - 2, scores, -1)
    top_vals, top_idx = lax.top_k(scores, 2)
    picks = jnp.where(top_vals >= 0, top_idx.astype(jnp.int32), NBLK)
    previous = jnp.where(row_ids >= 1, row_ids - 1, NBLK)
    return jnp.concatenate([row_ids, previous, picks], axis=1).astype(jnp.int32)


def level_of(stream_key, shape, cuts, smallest, largest):
    level, own = 1.0, jax.random.fold_in(stream_key, 6)
    for position, shards_of in cuts:
        steps = jnp.exp(jax.random.uniform(jax.random.fold_in(own, position), (shards_of,), jnp.float32, smallest / len(cuts), largest / len(cuts)))
        level = level * jnp.repeat(steps, shape[position] // shards_of).reshape([-1 if axis == position else 1 for axis in range(len(shape))])
    return level


def normal_values(rng, shape, deviation, reach, cuts=(), kind=jnp.bfloat16):
    factor_of = level_of(rng, shape, cuts, -0.22, 0.18) if cuts else 1.0
    drawn = jax.random.normal(rng, shape, jnp.float32) * deviation * factor_of
    return jnp.minimum(jnp.maximum(drawn, -reach), reach).astype(kind)


def setup_inputs(seed: int = 0, part: int = 0) -> dict:
    key_of = jax.random.split(jax.random.key(seed), 7)
    part_keys = jax.random.split(jax.random.fold_in(key_of[6], part), 7)
    tokens = draw_tokens(jax.random.fold_in(jax.random.fold_in(key_of[6], part), 71), part)
    norm_gain = jnp.clip(1.0 + 0.15 * jax.random.normal(key_of[1], (SECTIONS, D), jnp.float32), 0.25, 1.75).astype(jnp.bfloat16)
    query_weight = draw_query_weight(jax.random.fold_in(key_of[6], 71), part)
    kv_weight = draw_kv_weight(jax.random.fold_in(key_of[6], 71), part)
    out_weight = normal_values(key_of[4], (SECTIONS, HQ * HD, D), (HD * 4) ** -0.5, 0.25, ((0, 4), (2, 4)))
    window_blocks = draw_window_blocks(jax.random.fold_in(jax.random.fold_in(key_of[6], part), 71), part)
    return dict(tokens=tokens, norm_gain=norm_gain, query_weight=query_weight, kv_weight=kv_weight, out_weight=out_weight, window_blocks=window_blocks)


EPS = 1e-05
THETA = 500000.0
NEG = -1e+30

def rotate(u, positions):
    half = u.shape[-1] // 2
    index = jnp.arange(half).astype(jnp.float32)
    freq = jnp.power(jnp.float32(THETA), -2.0 * index / u.shape[-1])
    angle = positions[:, None] * freq[None, :]
    cosine = jnp.cos(angle)[:, None, :]
    sine = jnp.sin(angle)[:, None, :]
    first = u[..., :half]
    second = u[..., half:]
    return jnp.concatenate([first * cosine - second * sine, second * cosine + first * sine], axis=-1)

def reference(tokens, norm_gain, query_weight, kv_weight, out_weight, window_blocks):
    positions = jnp.arange(TOK).astype(jnp.float32)
    block_ids = jnp.arange(NBLK).astype(jnp.int32)
    listed = jnp.any(window_blocks[:, :, None] == block_ids[None, None, :], axis=1)
    token_ids = jnp.arange(TOK).astype(jnp.int32)
    token_blocks = token_ids // BLK
    visible = listed[token_blocks][:, token_blocks] & (token_ids[None, :] <= token_ids[:, None])
    group = HQ // KVH

    def layer(state, weights):
        gain, w_query, w_kv, w_out = weights
        wide = state.astype(jnp.float32)
        squares = lax.optimization_barrier(jnp.sum(wide * wide, axis=1))
        scale = lax.rsqrt(squares / D + EPS)
        normed = (wide * gain.astype(jnp.float32)[None, :] * scale[:, None]).astype(jnp.bfloat16)
        raw_query = jnp.dot(normed, w_query, preferred_element_type=jnp.float32)
        queries = rotate(raw_query.reshape(TOK, HQ, HD), positions).astype(jnp.bfloat16)
        pairs = jnp.dot(normed, w_kv, preferred_element_type=jnp.float32).astype(jnp.bfloat16)
        keys = rotate(pairs[:, :KVH * HD].astype(jnp.float32).reshape(TOK, KVH, HD), positions).astype(jnp.bfloat16)
        values = pairs[:, KVH * HD:].reshape(TOK, KVH, HD)
        keys_full = jnp.repeat(keys, group, axis=1)
        values_full = jnp.repeat(values, group, axis=1)
        scores = jnp.einsum('qhd,khd->hqk', queries.astype(jnp.float32), keys_full.astype(jnp.float32)) / math.sqrt(HD)
        scores = jnp.where(visible[None], scores, NEG)
        top = lax.optimization_barrier(jnp.max(scores, axis=-1, keepdims=True))
        weights_soft = jnp.where(visible[None], jnp.exp(scores - top), 0.0)
        denom = lax.optimization_barrier(jnp.sum(weights_soft, axis=-1))
        probs = weights_soft.astype(jnp.bfloat16)
        mixed = jnp.einsum('hqk,khd->qhd', probs.astype(jnp.float32), values_full.astype(jnp.float32))
        mixed = mixed / jnp.transpose(denom)[:, :, None]
        heads = mixed.astype(jnp.bfloat16).reshape(TOK, HQ * HD)
        result = (wide + jnp.dot(heads, w_out, preferred_element_type=jnp.float32)).astype(jnp.bfloat16)
        return (result, result)
    final, states = lax.scan(layer, tokens, (norm_gain, query_weight, kv_weight, out_weight))
    return states
```

```python
import functools
import math

import jax
import jax.numpy as jnp
import numpy as np
from jax import lax
from jax.experimental import pallas as pl
from jax.experimental.pallas import tpu as pltpu
from jax.sharding import PartitionSpec as P

D = 4096
HD = 128
HQ = 16
KVH = 4
SLICE = 48
SLICES = 4
BLK = 16


EPS = 1e-05
THETA = 500000.0
NEG = -1e30


def from_behind(value, axis, steps):
    count = lax.axis_size(axis)
    initial, last = (max(0, -steps), min(count, count - steps))
    return lax.ppermute(value, axis, [(source, source + steps) for source in range(initial, last)])


def rotate(u, positions):
    half = u.shape[-1] // 2
    index = jnp.arange(half).astype(jnp.float32)
    freq = jnp.power(jnp.float32(THETA), -2.0 * index / u.shape[-1])
    angle = positions[:, None] * freq[None, :]
    cosine = jnp.cos(angle)[:, None, :]
    sine = jnp.sin(angle)[:, None, :]
    first = u[..., :half]
    second = u[..., half:]
    return jnp.concatenate(
        [first * cosine - second * sine, second * cosine + first * sine], axis=-1
    )


def local(tokens, norm_gain, query_weight, kv_weight, out_weight, window_blocks):
    n_pipe = lax.axis_size("pipe")
    section = lax.axis_index("pipe")
    member = lax.axis_index("tensor")
    width = tokens.shape[1]
    total_tokens = tokens.shape[0]
    w_query = query_weight[0]
    w_kv = kv_weight[0]
    w_out = out_weight[0]
    gain = norm_gain[0]
    local_heads = w_query.shape[1] // HD
    group = HQ // KVH
    kv_head = member * local_heads // group
    nblocks = window_blocks.shape[0]
    block_ids = jnp.arange(nblocks, dtype=jnp.int32)
    listed = jnp.any(window_blocks[:, :, None] == block_ids[None, None, :], axis=1)
    key_pos = jnp.arange(total_tokens, dtype=jnp.int32)
    slice_blocks = SLICE // BLK
    ticks = SLICES + n_pipe - 1

    def project_rows(piece):
        return (
            jnp.dot(piece, w_query, preferred_element_type=jnp.float32),
            jnp.dot(piece, w_kv, preferred_element_type=jnp.float32),
        )

    def apply_out(piece):
        return jnp.dot(piece, w_out, preferred_element_type=jnp.float32)

    def tick(step, carry):
        incoming, key_cache, value_cache, states = carry
        index = step - section
        valid = (index >= 0) & (index < SLICES)
        slot = jnp.clip(index, 0, SLICES - 1)
        start = slot * SLICE
        fresh = lax.dynamic_slice_in_dim(tokens, start, SLICE, 0)
        current = jnp.where(section == 0, fresh, incoming)
        wide = current.astype(jnp.float32)
        squares = lax.psum(jnp.sum(wide * wide, axis=1), "tensor")
        scale = lax.rsqrt(squares / D + EPS)
        normed = (wide * gain.astype(jnp.float32)[None, :] * scale[:, None]).astype(jnp.bfloat16)
        raw_query, raw_kv = project_rows(lax.all_gather(normed, "tensor", axis=1, tiled=True))
        positions = (start + jnp.arange(SLICE, dtype=jnp.int32)).astype(jnp.float32)
        queries = rotate(raw_query.reshape(SLICE, local_heads, HD), positions).astype(jnp.bfloat16)
        pairs = lax.all_gather(raw_kv.astype(jnp.bfloat16), "tensor", axis=1, tiled=True)
        keys_new = lax.dynamic_slice_in_dim(pairs, kv_head * HD, HD, 1)
        values_new = lax.dynamic_slice_in_dim(pairs, (KVH + kv_head) * HD, HD, 1)
        keys_rot = rotate(keys_new.astype(jnp.float32)[:, None, :], positions)[:, 0, :].astype(
            jnp.bfloat16
        )
        keys_written = lax.dynamic_update_slice_in_dim(key_cache, keys_rot, start, 0)
        values_written = lax.dynamic_update_slice_in_dim(value_cache, values_new, start, 0)
        scores = jnp.einsum(
            "qhd,kd->hqk", queries, keys_written, preferred_element_type=jnp.float32
        ) / math.sqrt(HD)
        query_pos = start + jnp.arange(SLICE, dtype=jnp.int32)
        query_rows = lax.dynamic_slice_in_dim(listed, slot * slice_blocks, slice_blocks, 0)
        visible = jnp.repeat(jnp.repeat(query_rows, BLK, axis=0), BLK, axis=1)
        visible = visible & (key_pos[None, :] <= query_pos[:, None])
        scores = jnp.where(visible[None], scores, NEG)
        top = jnp.max(scores, axis=-1, keepdims=True)
        weights_soft = jnp.where(visible[None], jnp.exp(scores - top), 0.0)
        denom = jnp.sum(weights_soft, axis=-1)
        probs = weights_soft.astype(jnp.bfloat16)
        mixed = jnp.einsum("hqk,kd->qhd", probs, values_written, preferred_element_type=jnp.float32)
        mixed = mixed / jnp.transpose(denom)[:, :, None]
        heads = mixed.astype(jnp.bfloat16).reshape(SLICE, local_heads * HD)
        projected = apply_out(lax.all_gather(heads, "tensor", axis=1, tiled=True))
        result = (wide + projected).astype(jnp.bfloat16)
        states_written = lax.dynamic_update_slice_in_dim(states, result, start, 0)
        states = jnp.where(valid, states_written, states)
        key_cache = jnp.where(valid, keys_written, key_cache)
        value_cache = jnp.where(valid, values_written, value_cache)
        passed = from_behind(result, "pipe", 1)
        return (passed, key_cache, value_cache, states)

    initial_carry = (
        jnp.zeros((SLICE, width), jnp.bfloat16),
        jnp.zeros((total_tokens, HD), jnp.bfloat16),
        jnp.zeros((total_tokens, HD), jnp.bfloat16),
        jnp.zeros((total_tokens, width), jnp.bfloat16),
    )
    final_carry = lax.fori_loop(0, ticks, tick, initial_carry)
    return final_carry[3][None]


PIECES = 6
LANES = 128
MESH = pl.DeviceIdType.MESH
FORWARD, PROJECT, ATTEND, OUTPUT = range(4)
PACKED = 12
FIRST_MOVED = 2


def order_of(depths):
    stages = []
    for k in range(PIECES + max(depth for _, depth in depths)):
        for stage, depth in depths:
            if 0 <= k - depth < PIECES:
                stages.append(stage)
    return stages


ORDERS = (
    order_of(((FORWARD, 0), (PROJECT, 0), (ATTEND, 1), (OUTPUT, 2))),
    order_of(((FORWARD, 0), (PROJECT, 0), (ATTEND, 1), (OUTPUT, 2))),
    order_of(((FORWARD, 0), (PROJECT, 0), (ATTEND, 0), (OUTPUT, 1))),
)


def packed(stages):
    words = []
    for begin in range(0, len(stages), PACKED):
        words.append(sum(stage * 4**k for k, stage in enumerate(stages[begin : begin + PACKED])))
    return words


def relay_kernel(
    n_pipe,
    n_slices,
    window,
    tokens,
    gain,
    table,
    w_query,
    w_kv,
    w_out,
    out,
    turns,
    gain_row,
    queries,
    wq,
    wkv,
    wo,
    gains,
    seen,
    xg,
    normed,
    kv_send_buf,
    kv_in,
    keys,
    values,
    heads,
    w_sem,
    gain_send,
    gain_recv,
    x_recv,
    x_send,
    fwd_send,
    fwd_recv,
    kv_send,
    kv_recv,
    h_send,
    h_recv,
    wkv_send,
    wkv_recv,
):
    section = lax.axis_index("pipe")
    me = lax.axis_index("tensor")
    sibling = me + 1 - 2 * lax.rem(me, 2)
    across = lax.rem(me + 2, 4)
    diagonal = lax.rem(sibling + 2, 4)
    others = (sibling, across, diagonal)
    count, width = tokens.shape
    rows = count // n_slices
    padded = keys.shape[0]
    local_heads = wq.shape[1] // HD
    head_width = wq.shape[1]
    scale_scores = 1.0 / math.sqrt(HD)
    is_last = section == n_pipe - 1
    is_first = section == 0
    kind = me // 2
    moves_weights = section >= FIRST_MOVED
    direct = (jnp.where(is_first, me, sibling), jnp.where(is_first, diagonal, across))
    passed_on = (jnp.where(is_first, sibling, me), jnp.where(is_first, across, diagonal))

    def remote(src, dst, send, recv, target, pipe=None):
        where = {"tensor": target} if pipe is None else {"pipe": pipe, "tensor": target}
        return pltpu.make_async_remote_copy(
            src_ref=src, dst_ref=dst, send_sem=send, recv_sem=recv, device_id=where, device_id_type=MESH
        )

    kv_copy = pltpu.make_async_copy(w_kv, wkv.at[0], w_sem.at[0])
    query_copy = pltpu.make_async_copy(w_query, wq, w_sem.at[1])
    out_copy = pltpu.make_async_copy(w_out, wo, w_sem.at[2])
    table_copy = pltpu.make_async_copy(table, turns, w_sem.at[3])
    gain_load = pltpu.make_async_copy(gain, gain_row, w_sem.at[4])

    barrier = pltpu.get_barrier_semaphore()
    for peer in others:
        pl.semaphore_signal(barrier, inc=1, device_id={"tensor": peer}, device_id_type=MESH)

    @pl.when(jnp.logical_not(is_first))
    def _():
        for peer in (sibling, across):
            pl.semaphore_signal(
                barrier, inc=1, device_id={"pipe": section - 1, "tensor": peer}, device_id_type=MESH
            )

    @pl.when(jnp.logical_not(is_last))
    def _():
        for peer in (sibling, across):
            pl.semaphore_signal(
                barrier, inc=1, device_id={"pipe": section + 1, "tensor": peer}, device_id_type=MESH
            )

    for copy in (gain_load, kv_copy, query_copy, table_copy, out_copy):
        copy.start()
    @pl.when(is_first)
    def _():
        pltpu.make_async_copy(tokens, xg.at[me], x_recv.at[0, 0]).start()

    keys[...] = jnp.zeros_like(keys)
    values[...] = jnp.zeros_like(values)
    gain_load.wait()
    gains[me] = jnp.broadcast_to(gain_row[...].astype(jnp.float32), (8, width))
    expected = 7 - 2 * is_first.astype(jnp.int32) - 2 * is_last.astype(jnp.int32)
    pl.semaphore_wait(barrier, expected)

    def span(i):
        return pl.ds(pl.multiple_of(i * rows, BLK), rows)

    def sibling_tokens():
        return remote(tokens, xg.at[me], fwd_send.at[0, 0], fwd_recv.at[0, 0], sibling)

    def diagonal_tokens(i):
        part = span(i)
        return remote(tokens.at[part], xg.at[me, part], x_send.at[i, 1], x_recv.at[i, 1], diagonal)

    @pl.when(is_first)
    def _():
        diagonal_tokens(0).start()
        sibling_tokens().start()
        diagonal_tokens(1).start()

    def gain_copy(j):
        return remote(gains.at[me], gains.at[me], gain_send.at[j], gain_recv.at[j], others[j])

    for j in range(3):
        gain_copy(j).start()

    def x_copies(i):
        source, target = out.at[span(i)], xg.at[me, span(i)]
        return (
            remote(source, target, x_send.at[i, 0], x_recv.at[i, 0], sibling, section + 1),
            remote(source, target, x_send.at[i, 1], x_recv.at[i, 1], across, section + 1),
        )

    def forward(i, j):
        block = xg.at[direct[j], span(i)]
        return remote(block, block, fwd_send.at[i, j], fwd_recv.at[i, j], sibling)

    def heads_copy(i, j):
        return remote(heads.at[i, me], heads.at[i, me], h_send.at[i, j], h_recv.at[i, j], others[j])

    def kv_target(j):
        return lax.rem(2 * me + j, 4)

    def kv_remote(i, j, target):
        return remote(
            kv_send_buf.at[i, j], kv_in.at[i, kind], kv_send.at[i, j], kv_recv.at[i, kind], target
        )

    def weight_remote(j, target):
        return remote(
            w_kv.at[:, j * HD : (j + 1) * HD],
            wkv.at[1, :, pl.ds(pl.multiple_of(kind * HD, HD), HD)],
            wkv_send.at[j],
            wkv_recv.at[kind],
            target,
        )

    @pl.when(moves_weights)
    def _():
        for j in range(2):
            target = kv_target(j)

            @pl.when(target != me)
            def _():
                weight_remote(j, target).start()

            @pl.when(target == me)
            def _():
                pltpu.make_async_copy(
                    w_kv.at[:, j * HD : (j + 1) * HD],
                    wkv.at[1, :, pl.ds(pl.multiple_of(kind * HD, HD), HD)],
                    wkv_recv.at[kind],
                ).start()

    def arrived(dst, sem):
        pltpu.make_async_copy(dst, dst, sem).wait()

    column = lax.broadcasted_iota(jnp.int32, (BLK, padded), 1)
    row = lax.broadcasted_iota(jnp.int32, (BLK, padded), 0)
    column_block = column // BLK
    for block in range(n_slices * rows // BLK):
        listed = column_block == window[0, block]
        for j in range(1, 4):
            listed = listed | (column_block == window[j, block])
        causal = (column <= row + block * BLK) & (column < n_slices * rows)
        seen[block * BLK : (block + 1) * BLK, :] = jnp.where(listed & causal, 1.0, 0.0)

    key_part = (me < 2).astype(jnp.float32)

    def stage_forward(i):
        @pl.when(is_first)
        def _():
            @pl.when(i == 0)
            def _():
                arrived(xg.at[me], x_recv.at[0, 0])

            arrived(xg.at[diagonal, span(i)], x_recv.at[i, 1])
            forward(i, 1).start()

            @pl.when(i + 2 < n_slices)
            def _():
                diagonal_tokens(i + 2).start()

        @pl.when(jnp.logical_not(is_first))
        def _():
            for j in range(2):
                arrived(xg.at[direct[j], span(i)], x_recv.at[i, j])
                forward(i, j).start()

    def stage_project(i):
        @pl.when(i == 0)
        def _():
            for j in range(3):
                gain_copy(j).wait_recv()
            kv_copy.wait()
            query_copy.wait()
            table_copy.wait()

        @pl.when(moves_weights & (i == 0))
        def _():
            for c in range(2):
                block = wkv.at[1, :, c * HD : (c + 1) * HD]
                arrived(block, wkv_recv.at[c])

        slot = moves_weights.astype(jnp.int32)
        start = pl.multiple_of(i * rows, rows)
        cos = turns[pl.ds(start, rows), 0:HD]
        sin = turns[pl.ds(start, rows), HD : 2 * HD]

        def total_squares(sources):
            squares = jnp.zeros((rows, 1), jnp.float32)
            for s in sources:
                wide = xg[s, span(i), :].astype(jnp.float32)
                squares += jnp.sum(wide * wide, axis=1, keepdims=True)
            return squares

        def normalize(sources, scale):
            for s in sources:
                wide = xg[s, span(i), :].astype(jnp.float32)
                normed[s] = (wide * gains[s, 0:1, :] * scale).astype(jnp.bfloat16)

        def product(sources, weight):
            total = None
            for s in sources:
                begin = pl.multiple_of(s * width, width)
                term = jnp.dot(normed[s], weight(pl.ds(begin, width)), preferred_element_type=jnp.float32)
                total = term if total is None else total + term
            return total

        def kv_rows(span):
            return wkv[slot, span, :]

        def query_rows(span):
            return wq[span, :]

        near_squares = total_squares(direct)
        near_scale = lax.rsqrt(near_squares / (2 * width) + EPS)
        normalize(direct, near_scale)
        near_kv = product(direct, kv_rows)
        near_query = product(direct, query_rows)

        @pl.when(is_first & (i == 0))
        def _():
            arrived(xg.at[sibling], fwd_recv.at[0, 0])

        @pl.when(jnp.logical_not(is_first))
        def _():
            arrived(xg.at[passed_on[0], span(i)], fwd_recv.at[i, 0])

        arrived(xg.at[passed_on[1], span(i)], fwd_recv.at[i, 1])
        scale = lax.rsqrt((near_squares + total_squares(passed_on)) / (4 * width) + EPS)
        ratio = jnp.where(near_scale > 0.0, scale / near_scale, 0.0)
        normalize(passed_on, scale)
        raw_kv = near_kv * ratio + product(passed_on, kv_rows)
        pieces = []
        for j in range(2):
            turns_part = jnp.where(moves_weights, 1.0 - j, key_part)
            kv_cos = cos * turns_part + (1.0 - turns_part)
            kv_sin = sin * turns_part
            piece = raw_kv[:, j * HD : (j + 1) * HD].astype(jnp.bfloat16).astype(jnp.float32)
            turned = piece * kv_cos + pltpu.roll(piece, HD // 2, 1) * kv_sin
            pieces.append(turned.astype(jnp.bfloat16))

        @pl.when(moves_weights)
        def _():
            keys[pl.ds(start, rows), :] = pieces[0]
            values[pl.ds(start, rows), :] = pieces[1]

        @pl.when(jnp.logical_not(moves_weights))
        def _():
            for j in range(2):
                kv_send_buf[i, j] = pieces[j]
            for j in range(2):
                target = kv_target(j)

                @pl.when(target != me)
                def _():
                    kv_remote(i, j, target).start()

                @pl.when(target == me)
                def _():
                    kv_in[i, kind] = pieces[j]

        raw_query = near_query * ratio + product(passed_on, query_rows)
        turned = []
        for h in range(local_heads):
            u = raw_query[:, h * HD : (h + 1) * HD]
            turned.append((u * cos + pltpu.roll(u, HD // 2, 1) * sin).astype(jnp.bfloat16))
        queries[i] = jnp.concatenate(turned, axis=0)

    def stage_attend(i):
        start = pl.multiple_of(i * rows, rows)
        visible = jnp.concatenate([seen[pl.ds(start, rows), :]] * local_heads, axis=0) > 0.5

        @pl.when(jnp.logical_not(moves_weights))
        def _():
            for k in range(2):

                @pl.when(2 * k + me // 2 != me)
                def _():
                    arrived(kv_in.at[i, k], kv_recv.at[i, k])

            keys[pl.ds(start, rows), :] = kv_in[i, 0]
            values[pl.ds(start, rows), :] = kv_in[i, 1]

        scores = (
            lax.dot_general(
                queries[i], keys[...], (((1,), (1,)), ((), ())), preferred_element_type=jnp.float32
            )
            * scale_scores
        )
        scores = jnp.where(visible, scores, NEG)
        top = jnp.max(scores, axis=1, keepdims=True)
        weights = jnp.where(visible, jnp.exp(scores - top), 0.0)
        denom = jnp.sum(weights, axis=1, keepdims=True)
        mixed = jnp.dot(weights.astype(jnp.bfloat16), values[...], preferred_element_type=jnp.float32)
        mixed = (mixed / denom).astype(jnp.bfloat16)
        for h in range(local_heads):
            heads[i, me, :, h * HD : (h + 1) * HD] = mixed[h * rows : (h + 1) * rows, :]
        for j in (1, 2, 0):
            heads_copy(i, j).start()

    def stage_output(i):
        @pl.when(i == 0)
        def _():
            out_copy.wait()

        start = pl.multiple_of(i * rows, rows)
        total = xg[me, span(i), :].astype(jnp.float32)
        for j in (None, 0, 2, 1):
            source = me if j is None else others[j]
            if j is not None:
                arrived(heads.at[i, source], h_recv.at[i, j])
            begin = pl.multiple_of(source * head_width, head_width)
            total += jnp.dot(
                heads[i, source], wo[pl.ds(begin, head_width), :], preferred_element_type=jnp.float32
            )
        out[span(i), :] = total.astype(jnp.bfloat16)

        @pl.when(jnp.logical_not(is_last))
        def _():
            for copy in reversed(x_copies(i)):
                copy.start()


    orders = [packed(stages) for stages in ORDERS]

    def step(k, state):
        word, counts = state[0], state[1:]
        for w in range(len(orders[0])):
            fresh = jnp.where(section == 0, orders[0][w], jnp.where(section == 1, orders[1][w], orders[2][w]))
            word = jnp.where(k == w * PACKED, fresh, word)
        code = lax.rem(word, 4)
        for stage, run in enumerate((stage_forward, stage_project, stage_attend, stage_output)):

            @pl.when(code == stage)
            def _():
                run(counts[stage])

        after = [count + (code == stage).astype(jnp.int32) for stage, count in enumerate(counts)]
        return (word // 4, *after)

    lax.fori_loop(0, 4 * n_slices, step, (jnp.int32(0),) * 5)

    for j in range(3):
        gain_copy(j).wait_send()

    @pl.when(moves_weights)
    def _():
        for j in range(2):
            target = kv_target(j)

            @pl.when(target != me)
            def _():
                weight_remote(j, target).wait_send()

    @pl.when(is_first)
    def _():
        sibling_tokens().wait_send()

    @pl.loop(0, n_slices)
    def _(i):
        @pl.when(jnp.logical_not(is_last))
        def _():
            for copy in x_copies(i):
                copy.wait_send()

        @pl.when(is_first)
        def _():
            diagonal_tokens(i).wait_send()

        for j in range(2):

            @pl.when((j == 1) | jnp.logical_not(is_first))
            def _():
                forward(i, j).wait_send()

            target = kv_target(j)

            @pl.when((target != me) & jnp.logical_not(moves_weights))
            def _():
                kv_remote(i, j, target).wait_send()

        for j in range(3):
            heads_copy(i, j).wait_send()


def tables(count):
    index = np.arange(HD // 2, dtype=np.float32)
    freq = np.power(np.float32(THETA), np.float32(-2.0) * index / np.float32(HD)).astype(np.float32)
    angle = np.arange(count, dtype=np.float32)[:, None] * freq[None, :]
    cosine, sine = np.cos(angle), np.sin(angle)
    return np.concatenate([cosine, cosine, -sine, sine], axis=1).astype(np.float32)


def relay(n_pipe, tokens, norm_gain, query_weight, kv_weight, out_weight, window_blocks):
    count, width = tokens.shape
    n = PIECES
    rows = count // n
    w_query, w_kv, w_out = query_weight[0], kv_weight[0], out_weight[0]
    head_width = w_query.shape[1]
    padded = -(-count // LANES) * LANES
    anywhere = pl.BlockSpec(memory_space=pl.ANY)
    dma = pltpu.SemaphoreType.DMA
    states = pl.pallas_call(
        functools.partial(relay_kernel, n_pipe, n),
        out_shape=pltpu.VMEM((count, width), jnp.bfloat16),
        in_specs=[pl.BlockSpec(memory_space=pltpu.SMEM)] + [anywhere] * 6,
        out_specs=pl.BlockSpec(memory_space=pltpu.VMEM),
        scratch_shapes=[
            pltpu.VMEM((count, 2 * HD), jnp.float32),
            pltpu.VMEM((1, width), jnp.bfloat16),
            pltpu.VMEM((n, rows * (head_width // HD), HD), jnp.bfloat16),
            pltpu.VMEM(w_query.shape, jnp.bfloat16),
            pltpu.VMEM((2,) + w_kv.shape, jnp.bfloat16),
            pltpu.VMEM(w_out.shape, jnp.bfloat16),
            pltpu.VMEM((4, 8, width), jnp.float32),
            pltpu.VMEM((count, padded), jnp.float32),
            pltpu.VMEM((4, count, width), jnp.bfloat16),
            pltpu.VMEM((4, rows, width), jnp.bfloat16),
            pltpu.VMEM((n, 2, rows, HD), jnp.bfloat16),
            pltpu.VMEM((n, 2, rows, HD), jnp.bfloat16),
            pltpu.VMEM((padded, HD), jnp.bfloat16),
            pltpu.VMEM((padded, HD), jnp.bfloat16),
            pltpu.VMEM((n, 4, rows, head_width), jnp.bfloat16),
            dma((5,)),
            dma((3,)),
            dma((3,)),
            dma((n, 2)),
            dma((n, 2)),
            dma((n, 2)),
            dma((n, 2)),
            dma((n, 2)),
            dma((n, 2)),
            dma((n, 3)),
            dma((n, 3)),
            dma((2,)),
            dma((2,)),
        ],
        compiler_params=pltpu.CompilerParams(
            collective_id=0, has_side_effects=True, vmem_limit_bytes=56 * 1024 * 1024
        ),
        name="relay",
    )(window_blocks.T, tokens, norm_gain, tables(count), w_query, w_kv, w_out)
    return states[None]


def fits_relay(tokens, query_weight, kv_weight, n_tensor):
    return (
        n_tensor == 4
        and tokens.shape[0] % (PIECES * BLK) == 0
        and kv_weight.shape[2] == 2 * HD
        and query_weight.shape[2] == HQ * HD // 4
        and HQ // KVH == HQ // 4
    )


def program(n_pipe, n_tensor, *args):
    if fits_relay(args[0], args[2], args[3], n_tensor):
        return relay(n_pipe, *args)
    return local(*args)


def solution(mesh):
    placed = (
        P("seq", "tensor"),
        P("pipe", "tensor"),
        P("pipe", None, "tensor"),
        P("pipe", None, "tensor"),
        P("pipe", None, "tensor"),
        P("seq", None),
    )
    part = functools.partial(program, mesh.shape["pipe"], mesh.shape["tensor"])
    return jax.shard_map(
        part, mesh=mesh, in_specs=placed, out_specs=P("pipe", "seq", "tensor"), check_vma=False
    )
```

```python
import functools
import math

import jax
import jax.numpy as jnp
import numpy as np
from jax import lax
from jax.experimental import pallas as pl
from jax.experimental.pallas import tpu as pltpu
from jax.sharding import PartitionSpec as P

D = 4096
HD = 128
HQ = 16
KVH = 4
SLICE = 48
SLICES = 4
BLK = 16


EPS = 1e-05
THETA = 500000.0
NEG = -1e30


def from_behind(value, axis, steps):
    count = lax.axis_size(axis)
    initial, last = (max(0, -steps), min(count, count - steps))
    return lax.ppermute(value, axis, [(source, source + steps) for source in range(initial, last)])


def rotate(u, positions):
    half = u.shape[-1] // 2
    index = jnp.arange(half).astype(jnp.float32)
    freq = jnp.power(jnp.float32(THETA), -2.0 * index / u.shape[-1])
    angle = positions[:, None] * freq[None, :]
    cosine = jnp.cos(angle)[:, None, :]
    sine = jnp.sin(angle)[:, None, :]
    first = u[..., :half]
    second = u[..., half:]
    return jnp.concatenate(
        [first * cosine - second * sine, second * cosine + first * sine], axis=-1
    )


def local(tokens, norm_gain, query_weight, kv_weight, out_weight, window_blocks):
    n_pipe = lax.axis_size("pipe")
    section = lax.axis_index("pipe")
    member = lax.axis_index("tensor")
    width = tokens.shape[1]
    total_tokens = tokens.shape[0]
    w_query = query_weight[0]
    w_kv = kv_weight[0]
    w_out = out_weight[0]
    gain = norm_gain[0]
    local_heads = w_query.shape[1] // HD
    group = HQ // KVH
    kv_head = member * local_heads // group
    nblocks = window_blocks.shape[0]
    block_ids = jnp.arange(nblocks, dtype=jnp.int32)
    listed = jnp.any(window_blocks[:, :, None] == block_ids[None, None, :], axis=1)
    key_pos = jnp.arange(total_tokens, dtype=jnp.int32)
    slice_blocks = SLICE // BLK
    ticks = SLICES + n_pipe - 1

    def project_rows(piece):
        return (
            jnp.dot(piece, w_query, preferred_element_type=jnp.float32),
            jnp.dot(piece, w_kv, preferred_element_type=jnp.float32),
        )

    def apply_out(piece):
        return jnp.dot(piece, w_out, preferred_element_type=jnp.float32)

    def tick(step, carry):
        incoming, key_cache, value_cache, states = carry
        index = step - section
        valid = (index >= 0) & (index < SLICES)
        slot = jnp.clip(index, 0, SLICES - 1)
        start = slot * SLICE
        fresh = lax.dynamic_slice_in_dim(tokens, start, SLICE, 0)
        current = jnp.where(section == 0, fresh, incoming)
        wide = current.astype(jnp.float32)
        squares = lax.psum(jnp.sum(wide * wide, axis=1), "tensor")
        scale = lax.rsqrt(squares / D + EPS)
        normed = (wide * gain.astype(jnp.float32)[None, :] * scale[:, None]).astype(jnp.bfloat16)
        raw_query, raw_kv = project_rows(lax.all_gather(normed, "tensor", axis=1, tiled=True))
        positions = (start + jnp.arange(SLICE, dtype=jnp.int32)).astype(jnp.float32)
        queries = rotate(raw_query.reshape(SLICE, local_heads, HD), positions).astype(jnp.bfloat16)
        pairs = lax.all_gather(raw_kv.astype(jnp.bfloat16), "tensor", axis=1, tiled=True)
        keys_new = lax.dynamic_slice_in_dim(pairs, kv_head * HD, HD, 1)
        values_new = lax.dynamic_slice_in_dim(pairs, (KVH + kv_head) * HD, HD, 1)
        keys_rot = rotate(keys_new.astype(jnp.float32)[:, None, :], positions)[:, 0, :].astype(
            jnp.bfloat16
        )
        keys_written = lax.dynamic_update_slice_in_dim(key_cache, keys_rot, start, 0)
        values_written = lax.dynamic_update_slice_in_dim(value_cache, values_new, start, 0)
        scores = jnp.einsum(
            "qhd,kd->hqk", queries, keys_written, preferred_element_type=jnp.float32
        ) / math.sqrt(HD)
        query_pos = start + jnp.arange(SLICE, dtype=jnp.int32)
        query_rows = lax.dynamic_slice_in_dim(listed, slot * slice_blocks, slice_blocks, 0)
        visible = jnp.repeat(jnp.repeat(query_rows, BLK, axis=0), BLK, axis=1)
        visible = visible & (key_pos[None, :] <= query_pos[:, None])
        scores = jnp.where(visible[None], scores, NEG)
        top = jnp.max(scores, axis=-1, keepdims=True)
        weights_soft = jnp.where(visible[None], jnp.exp(scores - top), 0.0)
        denom = jnp.sum(weights_soft, axis=-1)
        probs = weights_soft.astype(jnp.bfloat16)
        mixed = jnp.einsum("hqk,kd->qhd", probs, values_written, preferred_element_type=jnp.float32)
        mixed = mixed / jnp.transpose(denom)[:, :, None]
        heads = mixed.astype(jnp.bfloat16).reshape(SLICE, local_heads * HD)
        projected = apply_out(lax.all_gather(heads, "tensor", axis=1, tiled=True))
        result = (wide + projected).astype(jnp.bfloat16)
        states_written = lax.dynamic_update_slice_in_dim(states, result, start, 0)
        states = jnp.where(valid, states_written, states)
        key_cache = jnp.where(valid, keys_written, key_cache)
        value_cache = jnp.where(valid, values_written, value_cache)
        passed = from_behind(result, "pipe", 1)
        return (passed, key_cache, value_cache, states)

    initial_carry = (
        jnp.zeros((SLICE, width), jnp.bfloat16),
        jnp.zeros((total_tokens, HD), jnp.bfloat16),
        jnp.zeros((total_tokens, HD), jnp.bfloat16),
        jnp.zeros((total_tokens, width), jnp.bfloat16),
    )
    final_carry = lax.fori_loop(0, ticks, tick, initial_carry)
    return final_carry[3][None]


PIECES = 6
LANES = 128
MESH = pl.DeviceIdType.MESH
FORWARD, PROJECT, ATTEND, OUTPUT = range(4)
PACKED = 12
FIRST_MOVED = 2
MOVED_AFTER = 0


def order_of(depths):
    stages = []
    for k in range(PIECES + max(depth for _, depth in depths)):
        for stage, depth in depths:
            if 0 <= k - depth < PIECES:
                stages.append(stage)
    return stages


ORDERS = (
    order_of(((OUTPUT, 3), (ATTEND, 2), (PROJECT, 1), (FORWARD, 0))),
    order_of(((OUTPUT, 3), (ATTEND, 2), (PROJECT, 1), (FORWARD, 0))),
    order_of(((FORWARD, 0), (PROJECT, 0), (ATTEND, 0), (OUTPUT, 1))),
)


def packed(stages):
    words = []
    for begin in range(0, len(stages), PACKED):
        words.append(sum(stage * 4**k for k, stage in enumerate(stages[begin : begin + PACKED])))
    return words


def relay_kernel(
    n_pipe,
    n_slices,
    window,
    tokens,
    gain,
    table,
    w_query,
    w_kv,
    w_out,
    out,
    turns,
    gain_row,
    queries,
    wq,
    wkv,
    wo,
    gains,
    seen,
    xg,
    normed,
    kv_send_buf,
    kv_in,
    keys,
    values,
    heads,
    w_sem,
    gain_send,
    gain_recv,
    x_recv,
    x_send,
    fwd_send,
    fwd_recv,
    kv_send,
    kv_recv,
    h_send,
    h_recv,
    wkv_send,
    wkv_recv,
):
    section = lax.axis_index("pipe")
    me = lax.axis_index("tensor")
    sibling = me + 1 - 2 * lax.rem(me, 2)
    across = lax.rem(me + 2, 4)
    diagonal = lax.rem(sibling + 2, 4)
    others = (sibling, across, diagonal)
    rows = xg.shape[2]
    width = xg.shape[3]
    padded = keys.shape[0]
    local_heads = wq.shape[1] // HD
    head_width = wq.shape[1]
    scale_scores = 1.0 / math.sqrt(HD)
    is_last = section == n_pipe - 1
    is_first = section == 0
    kind = me // 2
    moves_weights = section >= FIRST_MOVED
    first_moved = jnp.where(section >= 2, 0, MOVED_AFTER)
    direct = (jnp.where(is_first, me, sibling), jnp.where(is_first, diagonal, across))
    passed_on = (jnp.where(is_first, sibling, me), jnp.where(is_first, across, diagonal))

    def remote(src, dst, send, recv, target, pipe=None):
        where = {"tensor": target} if pipe is None else {"pipe": pipe, "tensor": target}
        return pltpu.make_async_remote_copy(
            src_ref=src, dst_ref=dst, send_sem=send, recv_sem=recv, device_id=where, device_id_type=MESH
        )

    kv_copy = pltpu.make_async_copy(w_kv, wkv.at[0], w_sem.at[0])
    query_copy = pltpu.make_async_copy(w_query, wq, w_sem.at[1])
    out_copy = pltpu.make_async_copy(w_out, wo, w_sem.at[2])
    table_copy = pltpu.make_async_copy(table, turns, w_sem.at[3])
    gain_load = pltpu.make_async_copy(gain, gain_row, w_sem.at[4])

    barrier = pltpu.get_barrier_semaphore()
    for peer in others:
        pl.semaphore_signal(barrier, inc=1, device_id={"tensor": peer}, device_id_type=MESH)

    @pl.when(jnp.logical_not(is_first))
    def _():
        for peer in (sibling, across):
            pl.semaphore_signal(
                barrier, inc=1, device_id={"pipe": section - 1, "tensor": peer}, device_id_type=MESH
            )

    @pl.when(jnp.logical_not(is_last))
    def _():
        for peer in (sibling, across):
            pl.semaphore_signal(
                barrier, inc=1, device_id={"pipe": section + 1, "tensor": peer}, device_id_type=MESH
            )

    for copy in (gain_load, kv_copy, query_copy, table_copy, out_copy):
        copy.start()
    keys[...] = jnp.zeros_like(keys)
    values[...] = jnp.zeros_like(values)
    gain_load.wait()
    gains[me] = jnp.broadcast_to(gain_row[...].astype(jnp.float32), (8, width))
    expected = 7 - 2 * is_first.astype(jnp.int32) - 2 * is_last.astype(jnp.int32)
    pl.semaphore_wait(barrier, expected)

    def own_tokens(i):
        return pltpu.make_async_copy(
            tokens.at[pl.ds(i * rows, rows)], xg.at[i, me], x_recv.at[i, 0]
        )

    def diagonal_tokens(i):
        return remote(
            tokens.at[pl.ds(i * rows, rows)], xg.at[i, me], x_send.at[i, 1], x_recv.at[i, 1], diagonal
        )

    @pl.when(is_first)
    def _():
        for i in range(2):
            diagonal_tokens(i).start()
            own_tokens(i).start()

    def gain_copy(j):
        return remote(gains.at[me], gains.at[me], gain_send.at[j], gain_recv.at[j], others[j])

    for j in range(3):
        gain_copy(j).start()

    def x_copies(i):
        return (
            remote(out.at[pl.ds(pl.multiple_of(i * rows, BLK), rows)], xg.at[i, me], x_send.at[i, 0], x_recv.at[i, 0], sibling, section + 1),
            remote(out.at[pl.ds(pl.multiple_of(i * rows, BLK), rows)], xg.at[i, me], x_send.at[i, 1], x_recv.at[i, 1], across, section + 1),
        )

    def forward(i, j):
        source = direct[j]
        return remote(xg.at[i, source], xg.at[i, source], fwd_send.at[i, j], fwd_recv.at[i, j], sibling)

    def heads_copy(i, j):
        return remote(heads.at[i, me], heads.at[i, me], h_send.at[i, j], h_recv.at[i, j], others[j])

    def kv_target(j):
        return lax.rem(2 * me + j, 4)

    def kv_remote(i, j, target):
        return remote(
            kv_send_buf.at[i, j], kv_in.at[i, kind], kv_send.at[i, j], kv_recv.at[i, kind], target
        )

    def weight_remote(j, target):
        return remote(
            w_kv.at[:, j * HD : (j + 1) * HD],
            wkv.at[1, :, pl.ds(pl.multiple_of(kind * HD, HD), HD)],
            wkv_send.at[j],
            wkv_recv.at[kind],
            target,
        )

    @pl.when(moves_weights)
    def _():
        for j in range(2):
            target = kv_target(j)

            @pl.when(target != me)
            def _():
                weight_remote(j, target).start()

            @pl.when(target == me)
            def _():
                pltpu.make_async_copy(
                    w_kv.at[:, j * HD : (j + 1) * HD],
                    wkv.at[1, :, pl.ds(pl.multiple_of(kind * HD, HD), HD)],
                    wkv_recv.at[kind],
                ).start()

    def arrived(dst, sem):
        pltpu.make_async_copy(dst, dst, sem).wait()

    column = lax.broadcasted_iota(jnp.int32, (BLK, padded), 1)
    row = lax.broadcasted_iota(jnp.int32, (BLK, padded), 0)
    column_block = column // BLK
    for block in range(n_slices * rows // BLK):
        listed = column_block == window[0, block]
        for j in range(1, 4):
            listed = listed | (column_block == window[j, block])
        causal = (column <= row + block * BLK) & (column < n_slices * rows)
        seen[block * BLK : (block + 1) * BLK, :] = jnp.where(listed & causal, 1.0, 0.0)

    key_part = (me < 2).astype(jnp.float32)

    def stage_forward(i):
        for j in range(2):
            arrived(xg.at[i, direct[j]], x_recv.at[i, j])
            forward(i, j).start()

        @pl.when(is_first & (i + 2 < n_slices))
        def _():
            diagonal_tokens(i + 2).start()
            own_tokens(i + 2).start()

    def stage_project(i):
        @pl.when(i == 0)
        def _():
            for j in range(3):
                gain_copy(j).wait_recv()
            kv_copy.wait()
            query_copy.wait()
            table_copy.wait()

        @pl.when(moves_weights & (i == first_moved))
        def _():
            for c in range(2):
                block = wkv.at[1, :, c * HD : (c + 1) * HD]
                arrived(block, wkv_recv.at[c])

        own_kv = moves_weights & (i >= first_moved)
        slot = own_kv.astype(jnp.int32)
        start = pl.multiple_of(i * rows, rows)
        cos = turns[pl.ds(start, rows), 0:HD]
        sin = turns[pl.ds(start, rows), HD : 2 * HD]

        def total_squares(sources):
            squares = jnp.zeros((rows, 1), jnp.float32)
            for s in sources:
                wide = xg[i, s].astype(jnp.float32)
                squares += jnp.sum(wide * wide, axis=1, keepdims=True)
            return squares

        def normalize(sources, scale):
            for s in sources:
                wide = xg[i, s].astype(jnp.float32)
                normed[s] = (wide * gains[s, 0:1, :] * scale).astype(jnp.bfloat16)

        def product(sources, weight):
            total = None
            for s in sources:
                begin = pl.multiple_of(s * width, width)
                term = jnp.dot(normed[s], weight(pl.ds(begin, width)), preferred_element_type=jnp.float32)
                total = term if total is None else total + term
            return total

        def kv_rows(span):
            return wkv[slot, span, :]

        def query_rows(span):
            return wq[span, :]

        near_squares = total_squares(direct)
        near_scale = lax.rsqrt(near_squares / (2 * width) + EPS)
        normalize(direct, near_scale)
        near_kv = product(direct, kv_rows)
        near_query = product(direct, query_rows)
        for j in range(2):
            arrived(xg.at[i, passed_on[j]], fwd_recv.at[i, j])
        scale = lax.rsqrt((near_squares + total_squares(passed_on)) / (4 * width) + EPS)
        ratio = jnp.where(near_scale > 0.0, scale / near_scale, 0.0)
        normalize(passed_on, scale)
        raw_kv = near_kv * ratio + product(passed_on, kv_rows)
        pieces = []
        for j in range(2):
            turns_part = jnp.where(own_kv, 1.0 - j, key_part)
            kv_cos = cos * turns_part + (1.0 - turns_part)
            kv_sin = sin * turns_part
            piece = raw_kv[:, j * HD : (j + 1) * HD].astype(jnp.bfloat16).astype(jnp.float32)
            turned = piece * kv_cos + pltpu.roll(piece, HD // 2, 1) * kv_sin
            pieces.append(turned.astype(jnp.bfloat16))

        @pl.when(own_kv)
        def _():
            keys[pl.ds(start, rows), :] = pieces[0]
            values[pl.ds(start, rows), :] = pieces[1]

        @pl.when(jnp.logical_not(own_kv))
        def _():
            for j in range(2):
                kv_send_buf[i, j] = pieces[j]
            for j in range(2):
                target = kv_target(j)

                @pl.when(target != me)
                def _():
                    kv_remote(i, j, target).start()

                @pl.when(target == me)
                def _():
                    pltpu.make_async_copy(
                        kv_send_buf.at[i, j], kv_in.at[i, kind], kv_recv.at[i, kind]
                    ).start()

        raw_query = near_query * ratio + product(passed_on, query_rows)
        turned = []
        for h in range(local_heads):
            u = raw_query[:, h * HD : (h + 1) * HD]
            turned.append((u * cos + pltpu.roll(u, HD // 2, 1) * sin).astype(jnp.bfloat16))
        queries[i] = jnp.concatenate(turned, axis=0)

    def stage_attend(i):
        start = pl.multiple_of(i * rows, rows)
        visible = jnp.concatenate([seen[pl.ds(start, rows), :]] * local_heads, axis=0) > 0.5

        @pl.when(jnp.logical_not(moves_weights & (i >= first_moved)))
        def _():
            for k in range(2):
                arrived(kv_in.at[i, k], kv_recv.at[i, k])
            keys[pl.ds(start, rows), :] = kv_in[i, 0]
            values[pl.ds(start, rows), :] = kv_in[i, 1]

        scores = (
            lax.dot_general(
                queries[i], keys[...], (((1,), (1,)), ((), ())), preferred_element_type=jnp.float32
            )
            * scale_scores
        )
        scores = jnp.where(visible, scores, NEG)
        top = jnp.max(scores, axis=1, keepdims=True)
        weights = jnp.where(visible, jnp.exp(scores - top), 0.0)
        denom = jnp.sum(weights, axis=1, keepdims=True)
        mixed = jnp.dot(weights.astype(jnp.bfloat16), values[...], preferred_element_type=jnp.float32)
        mixed = (mixed / denom).astype(jnp.bfloat16)
        for h in range(local_heads):
            heads[i, me, :, h * HD : (h + 1) * HD] = mixed[h * rows : (h + 1) * rows, :]
        for j in (1, 2, 0):
            heads_copy(i, j).start()

    def stage_output(i):
        @pl.when(i == 0)
        def _():
            out_copy.wait()

        start = pl.multiple_of(i * rows, rows)
        total = xg[i, me].astype(jnp.float32)
        for j in (None, 0, 2, 1):
            source = me if j is None else others[j]
            if j is not None:
                arrived(heads.at[i, source], h_recv.at[i, j])
            begin = pl.multiple_of(source * head_width, head_width)
            total += jnp.dot(
                heads[i, source], wo[pl.ds(begin, head_width), :], preferred_element_type=jnp.float32
            )
        out[pl.ds(pl.multiple_of(i * rows, BLK), rows), :] = total.astype(jnp.bfloat16)

        @pl.when(jnp.logical_not(is_last))
        def _():
            for copy in reversed(x_copies(i)):
                copy.start()


    orders = [packed(stages) for stages in ORDERS]

    def step(k, state):
        word, counts = state[0], state[1:]
        for w in range(len(orders[0])):
            fresh = jnp.where(section == 0, orders[0][w], jnp.where(section == 1, orders[1][w], orders[2][w]))
            word = jnp.where(k == w * PACKED, fresh, word)
        code = lax.rem(word, 4)
        for stage, run in enumerate((stage_forward, stage_project, stage_attend, stage_output)):

            @pl.when(code == stage)
            def _():
                run(counts[stage])

        after = [count + (code == stage).astype(jnp.int32) for stage, count in enumerate(counts)]
        return (word // 4, *after)

    lax.fori_loop(0, 4 * n_slices, step, (jnp.int32(0),) * 5)

    for j in range(3):
        gain_copy(j).wait_send()

    @pl.when(moves_weights)
    def _():
        for j in range(2):
            target = kv_target(j)

            @pl.when(target != me)
            def _():
                weight_remote(j, target).wait_send()

    @pl.loop(0, n_slices)
    def _(i):
        @pl.when(is_first)
        def _():
            diagonal_tokens(i).wait_send()

        @pl.when(jnp.logical_not(is_last))
        def _():
            for copy in x_copies(i):
                copy.wait_send()

        for j in range(2):
            forward(i, j).wait_send()
            target = kv_target(j)

            @pl.when((target != me) & jnp.logical_not(moves_weights & (i >= first_moved)))
            def _():
                kv_remote(i, j, target).wait_send()

        for j in range(3):
            heads_copy(i, j).wait_send()


def tables(count):
    index = np.arange(HD // 2, dtype=np.float32)
    freq = np.power(np.float32(THETA), np.float32(-2.0) * index / np.float32(HD)).astype(np.float32)
    angle = np.arange(count, dtype=np.float32)[:, None] * freq[None, :]
    cosine, sine = np.cos(angle), np.sin(angle)
    return np.concatenate([cosine, cosine, -sine, sine], axis=1).astype(np.float32)


def relay(n_pipe, tokens, norm_gain, query_weight, kv_weight, out_weight, window_blocks):
    count, width = tokens.shape
    n = PIECES
    rows = count // n
    w_query, w_kv, w_out = query_weight[0], kv_weight[0], out_weight[0]
    head_width = w_query.shape[1]
    padded = -(-count // LANES) * LANES
    anywhere = pl.BlockSpec(memory_space=pl.ANY)
    dma = pltpu.SemaphoreType.DMA
    states = pl.pallas_call(
        functools.partial(relay_kernel, n_pipe, n),
        out_shape=pltpu.VMEM((count, width), jnp.bfloat16),
        in_specs=[pl.BlockSpec(memory_space=pltpu.SMEM)] + [anywhere] * 6,
        out_specs=pl.BlockSpec(memory_space=pltpu.VMEM),
        scratch_shapes=[
            pltpu.VMEM((count, 2 * HD), jnp.float32),
            pltpu.VMEM((1, width), jnp.bfloat16),
            pltpu.VMEM((n, rows * (head_width // HD), HD), jnp.bfloat16),
            pltpu.VMEM(w_query.shape, jnp.bfloat16),
            pltpu.VMEM((2,) + w_kv.shape, jnp.bfloat16),
            pltpu.VMEM(w_out.shape, jnp.bfloat16),
            pltpu.VMEM((4, 8, width), jnp.float32),
            pltpu.VMEM((count, padded), jnp.float32),
            pltpu.VMEM((n, 4, rows, width), jnp.bfloat16),
            pltpu.VMEM((4, rows, width), jnp.bfloat16),
            pltpu.VMEM((n, 2, rows, HD), jnp.bfloat16),
            pltpu.VMEM((n, 2, rows, HD), jnp.bfloat16),
            pltpu.VMEM((padded, HD), jnp.bfloat16),
            pltpu.VMEM((padded, HD), jnp.bfloat16),
            pltpu.VMEM((n, 4, rows, head_width), jnp.bfloat16),
            dma((5,)),
            dma((3,)),
            dma((3,)),
            dma((n, 2)),
            dma((n, 2)),
            dma((n, 2)),
            dma((n, 2)),
            dma((n, 2)),
            dma((n, 2)),
            dma((n, 3)),
            dma((n, 3)),
            dma((2,)),
            dma((2,)),
        ],
        compiler_params=pltpu.CompilerParams(
            collective_id=0, has_side_effects=True, vmem_limit_bytes=56 * 1024 * 1024
        ),
        name="relay",
    )(window_blocks.T, tokens, norm_gain, tables(count), w_query, w_kv, w_out)
    return states[None]


def fits_relay(tokens, query_weight, kv_weight, n_tensor):
    return (
        n_tensor == 4
        and tokens.shape[0] % (PIECES * BLK) == 0
        and kv_weight.shape[2] == 2 * HD
        and query_weight.shape[2] == HQ * HD // 4
        and HQ // KVH == HQ // 4
    )


def program(n_pipe, n_tensor, *args):
    if fits_relay(args[0], args[2], args[3], n_tensor):
        return relay(n_pipe, *args)
    return local(*args)


def solution(mesh):
    placed = (
        P("seq", "tensor"),
        P("pipe", "tensor"),
        P("pipe", None, "tensor"),
        P("pipe", None, "tensor"),
        P("pipe", None, "tensor"),
        P("seq", None),
    )
    part = functools.partial(program, mesh.shape["pipe"], mesh.shape["tensor"])
    return jax.shard_map(
        part, mesh=mesh, in_specs=placed, out_specs=P("pipe", "seq", "tensor"), check_vma=False
    )
```

```python
import functools
import math

import jax
import jax.numpy as jnp
import numpy as np
from jax import lax
from jax.experimental import pallas as pl
from jax.experimental.pallas import tpu as pltpu
from jax.sharding import PartitionSpec as P

D = 4096
HD = 128
HQ = 16
KVH = 4
SLICE = 48
SLICES = 4
BLK = 16


EPS = 1e-05
THETA = 500000.0
NEG = -1e30


def from_behind(value, axis, steps):
    count = lax.axis_size(axis)
    initial, last = (max(0, -steps), min(count, count - steps))
    return lax.ppermute(value, axis, [(source, source + steps) for source in range(initial, last)])


def rotate(u, positions):
    half = u.shape[-1] // 2
    index = jnp.arange(half).astype(jnp.float32)
    freq = jnp.power(jnp.float32(THETA), -2.0 * index / u.shape[-1])
    angle = positions[:, None] * freq[None, :]
    cosine = jnp.cos(angle)[:, None, :]
    sine = jnp.sin(angle)[:, None, :]
    first = u[..., :half]
    second = u[..., half:]
    return jnp.concatenate(
        [first * cosine - second * sine, second * cosine + first * sine], axis=-1
    )


def local(tokens, norm_gain, query_weight, kv_weight, out_weight, window_blocks):
    n_pipe = lax.axis_size("pipe")
    section = lax.axis_index("pipe")
    member = lax.axis_index("tensor")
    width = tokens.shape[1]
    total_tokens = tokens.shape[0]
    w_query = query_weight[0]
    w_kv = kv_weight[0]
    w_out = out_weight[0]
    gain = norm_gain[0]
    local_heads = w_query.shape[1] // HD
    group = HQ // KVH
    kv_head = member * local_heads // group
    nblocks = window_blocks.shape[0]
    block_ids = jnp.arange(nblocks, dtype=jnp.int32)
    listed = jnp.any(window_blocks[:, :, None] == block_ids[None, None, :], axis=1)
    key_pos = jnp.arange(total_tokens, dtype=jnp.int32)
    slice_blocks = SLICE // BLK
    ticks = SLICES + n_pipe - 1

    def project_rows(piece):
        return (
            jnp.dot(piece, w_query, preferred_element_type=jnp.float32),
            jnp.dot(piece, w_kv, preferred_element_type=jnp.float32),
        )

    def apply_out(piece):
        return jnp.dot(piece, w_out, preferred_element_type=jnp.float32)

    def tick(step, carry):
        incoming, key_cache, value_cache, states = carry
        index = step - section
        valid = (index >= 0) & (index < SLICES)
        slot = jnp.clip(index, 0, SLICES - 1)
        start = slot * SLICE
        fresh = lax.dynamic_slice_in_dim(tokens, start, SLICE, 0)
        current = jnp.where(section == 0, fresh, incoming)
        wide = current.astype(jnp.float32)
        squares = lax.psum(jnp.sum(wide * wide, axis=1), "tensor")
        scale = lax.rsqrt(squares / D + EPS)
        normed = (wide * gain.astype(jnp.float32)[None, :] * scale[:, None]).astype(jnp.bfloat16)
        raw_query, raw_kv = project_rows(lax.all_gather(normed, "tensor", axis=1, tiled=True))
        positions = (start + jnp.arange(SLICE, dtype=jnp.int32)).astype(jnp.float32)
        queries = rotate(raw_query.reshape(SLICE, local_heads, HD), positions).astype(jnp.bfloat16)
        pairs = lax.all_gather(raw_kv.astype(jnp.bfloat16), "tensor", axis=1, tiled=True)
        keys_new = lax.dynamic_slice_in_dim(pairs, kv_head * HD, HD, 1)
        values_new = lax.dynamic_slice_in_dim(pairs, (KVH + kv_head) * HD, HD, 1)
        keys_rot = rotate(keys_new.astype(jnp.float32)[:, None, :], positions)[:, 0, :].astype(
            jnp.bfloat16
        )
        keys_written = lax.dynamic_update_slice_in_dim(key_cache, keys_rot, start, 0)
        values_written = lax.dynamic_update_slice_in_dim(value_cache, values_new, start, 0)
        scores = jnp.einsum(
            "qhd,kd->hqk", queries, keys_written, preferred_element_type=jnp.float32
        ) / math.sqrt(HD)
        query_pos = start + jnp.arange(SLICE, dtype=jnp.int32)
        query_rows = lax.dynamic_slice_in_dim(listed, slot * slice_blocks, slice_blocks, 0)
        visible = jnp.repeat(jnp.repeat(query_rows, BLK, axis=0), BLK, axis=1)
        visible = visible & (key_pos[None, :] <= query_pos[:, None])
        scores = jnp.where(visible[None], scores, NEG)
        top = jnp.max(scores, axis=-1, keepdims=True)
        weights_soft = jnp.where(visible[None], jnp.exp(scores - top), 0.0)
        denom = jnp.sum(weights_soft, axis=-1)
        probs = weights_soft.astype(jnp.bfloat16)
        mixed = jnp.einsum("hqk,kd->qhd", probs, values_written, preferred_element_type=jnp.float32)
        mixed = mixed / jnp.transpose(denom)[:, :, None]
        heads = mixed.astype(jnp.bfloat16).reshape(SLICE, local_heads * HD)
        projected = apply_out(lax.all_gather(heads, "tensor", axis=1, tiled=True))
        result = (wide + projected).astype(jnp.bfloat16)
        states_written = lax.dynamic_update_slice_in_dim(states, result, start, 0)
        states = jnp.where(valid, states_written, states)
        key_cache = jnp.where(valid, keys_written, key_cache)
        value_cache = jnp.where(valid, values_written, value_cache)
        passed = from_behind(result, "pipe", 1)
        return (passed, key_cache, value_cache, states)

    initial_carry = (
        jnp.zeros((SLICE, width), jnp.bfloat16),
        jnp.zeros((total_tokens, HD), jnp.bfloat16),
        jnp.zeros((total_tokens, HD), jnp.bfloat16),
        jnp.zeros((total_tokens, width), jnp.bfloat16),
    )
    final_carry = lax.fori_loop(0, ticks, tick, initial_carry)
    return final_carry[3][None]


PIECES = 6
LANES = 128
MESH = pl.DeviceIdType.MESH
FORWARD, PROJECT, ATTEND, OUTPUT = range(4)
PACKED = 12
FIRST_MOVED = 2
MOVED_AFTER = 0


ORDERS = tuple(
    ["FPAO".index(stage) for stage in order]
    for order in (
        "FPFAPFOAPFFOAPOAPFOAPOAO",
        "FPFAPFOAPOFAPFOAPFOAPOAO",
        "FPAFPAOFPAOFPAOFPOAFPAOO",
        "FPAFPAOFPAOFPAOFPOFAPAOO",
    )
)


def packed(stages):
    words = []
    for begin in range(0, len(stages), PACKED):
        words.append(sum(stage * 4**k for k, stage in enumerate(stages[begin : begin + PACKED])))
    return words


def relay_kernel(
    n_pipe,
    n_slices,
    window,
    tokens,
    gain,
    table,
    w_query,
    w_kv,
    w_out,
    out,
    turns,
    gain_row,
    queries,
    wq,
    wkv,
    wo,
    gains,
    seen,
    xg,
    normed,
    kv_send_buf,
    kv_in,
    keys,
    values,
    heads,
    w_sem,
    gain_send,
    gain_recv,
    x_recv,
    x_send,
    fwd_send,
    fwd_recv,
    kv_send,
    kv_recv,
    h_send,
    h_recv,
    wkv_send,
    wkv_recv,
):
    section = lax.axis_index("pipe")
    me = lax.axis_index("tensor")
    sibling = me + 1 - 2 * lax.rem(me, 2)
    across = lax.rem(me + 2, 4)
    diagonal = lax.rem(sibling + 2, 4)
    others = (sibling, across, diagonal)
    rows = xg.shape[2]
    width = xg.shape[3]
    padded = keys.shape[0]
    local_heads = wq.shape[1] // HD
    head_width = wq.shape[1]
    scale_scores = 1.0 / math.sqrt(HD)
    is_last = section == n_pipe - 1
    is_first = section == 0
    kind = me // 2
    moves_weights = section >= FIRST_MOVED
    first_moved = jnp.where(section >= 2, 0, MOVED_AFTER)
    direct = (jnp.where(is_first, me, sibling), jnp.where(is_first, diagonal, across))
    passed_on = (jnp.where(is_first, sibling, me), jnp.where(is_first, across, diagonal))

    def remote(src, dst, send, recv, target, pipe=None):
        where = {"tensor": target} if pipe is None else {"pipe": pipe, "tensor": target}
        return pltpu.make_async_remote_copy(
            src_ref=src, dst_ref=dst, send_sem=send, recv_sem=recv, device_id=where, device_id_type=MESH
        )

    kv_copy = pltpu.make_async_copy(w_kv, wkv.at[0], w_sem.at[0])
    query_copy = pltpu.make_async_copy(w_query, wq, w_sem.at[1])
    out_copy = pltpu.make_async_copy(w_out, wo, w_sem.at[2])
    table_copy = pltpu.make_async_copy(table, turns, w_sem.at[3])
    gain_load = pltpu.make_async_copy(gain, gain_row, w_sem.at[4])

    barrier = pltpu.get_barrier_semaphore()
    for peer in others:
        pl.semaphore_signal(barrier, inc=1, device_id={"tensor": peer}, device_id_type=MESH)

    @pl.when(jnp.logical_not(is_first))
    def _():
        for peer in (sibling, across):
            pl.semaphore_signal(
                barrier, inc=1, device_id={"pipe": section - 1, "tensor": peer}, device_id_type=MESH
            )

    @pl.when(jnp.logical_not(is_last))
    def _():
        for peer in (sibling, across):
            pl.semaphore_signal(
                barrier, inc=1, device_id={"pipe": section + 1, "tensor": peer}, device_id_type=MESH
            )

    for copy in (gain_load, kv_copy, query_copy, table_copy, out_copy):
        copy.start()
    keys[...] = jnp.zeros_like(keys)
    values[...] = jnp.zeros_like(values)
    gain_load.wait()
    gains[me] = jnp.broadcast_to(gain_row[...].astype(jnp.float32), (8, width))
    expected = 7 - 2 * is_first.astype(jnp.int32) - 2 * is_last.astype(jnp.int32)
    pl.semaphore_wait(barrier, expected)

    def own_tokens(i):
        return pltpu.make_async_copy(
            tokens.at[pl.ds(i * rows, rows)], xg.at[i, me], x_recv.at[i, 0]
        )

    def diagonal_tokens(i):
        return remote(
            tokens.at[pl.ds(i * rows, rows)], xg.at[i, me], x_send.at[i, 1], x_recv.at[i, 1], diagonal
        )

    @pl.when(is_first)
    def _():
        for i in range(2):
            diagonal_tokens(i).start()
            own_tokens(i).start()

    def gain_copy(j):
        return remote(gains.at[me], gains.at[me], gain_send.at[j], gain_recv.at[j], others[j])

    for j in range(3):
        gain_copy(j).start()

    def x_copies(i):
        return (
            remote(out.at[pl.ds(pl.multiple_of(i * rows, BLK), rows)], xg.at[i, me], x_send.at[i, 0], x_recv.at[i, 0], sibling, section + 1),
            remote(out.at[pl.ds(pl.multiple_of(i * rows, BLK), rows)], xg.at[i, me], x_send.at[i, 1], x_recv.at[i, 1], across, section + 1),
        )

    def forward(i, j):
        source = direct[j]
        return remote(xg.at[i, source], xg.at[i, source], fwd_send.at[i, j], fwd_recv.at[i, j], sibling)

    def heads_copy(i, j):
        return remote(heads.at[i, me], heads.at[i, me], h_send.at[i, j], h_recv.at[i, j], others[j])

    def kv_target(j):
        return lax.rem(2 * me + j, 4)

    def kv_remote(i, j, target):
        return remote(
            kv_send_buf.at[i, j], kv_in.at[i, kind], kv_send.at[i, j], kv_recv.at[i, kind], target
        )

    def weight_remote(j, target):
        return remote(
            w_kv.at[:, j * HD : (j + 1) * HD],
            wkv.at[1, :, pl.ds(pl.multiple_of(kind * HD, HD), HD)],
            wkv_send.at[j],
            wkv_recv.at[kind],
            target,
        )

    @pl.when(moves_weights)
    def _():
        for j in range(2):
            target = kv_target(j)

            @pl.when(target != me)
            def _():
                weight_remote(j, target).start()

            @pl.when(target == me)
            def _():
                pltpu.make_async_copy(
                    w_kv.at[:, j * HD : (j + 1) * HD],
                    wkv.at[1, :, pl.ds(pl.multiple_of(kind * HD, HD), HD)],
                    wkv_recv.at[kind],
                ).start()

    def arrived(dst, sem):
        pltpu.make_async_copy(dst, dst, sem).wait()

    column = lax.broadcasted_iota(jnp.int32, (BLK, padded), 1)
    row = lax.broadcasted_iota(jnp.int32, (BLK, padded), 0)
    column_block = column // BLK
    for block in range(n_slices * rows // BLK):
        listed = column_block == window[0, block]
        for j in range(1, 4):
            listed = listed | (column_block == window[j, block])
        causal = (column <= row + block * BLK) & (column < n_slices * rows)
        seen[block * BLK : (block + 1) * BLK, :] = jnp.where(listed & causal, 1.0, 0.0)

    key_part = (me < 2).astype(jnp.float32)

    def stage_forward(i):
        for j in range(2):
            arrived(xg.at[i, direct[j]], x_recv.at[i, j])
            forward(i, j).start()

        @pl.when(is_first & (i + 2 < n_slices))
        def _():
            diagonal_tokens(i + 2).start()
            own_tokens(i + 2).start()

    def stage_project(i):
        @pl.when(i == 0)
        def _():
            for j in range(3):
                gain_copy(j).wait_recv()
            kv_copy.wait()
            query_copy.wait()
            table_copy.wait()

        @pl.when(moves_weights & (i == first_moved))
        def _():
            for c in range(2):
                block = wkv.at[1, :, c * HD : (c + 1) * HD]
                arrived(block, wkv_recv.at[c])

        own_kv = moves_weights & (i >= first_moved)
        slot = own_kv.astype(jnp.int32)
        start = pl.multiple_of(i * rows, rows)
        cos = turns[pl.ds(start, rows), 0:HD]
        sin = turns[pl.ds(start, rows), HD : 2 * HD]

        def total_squares(sources):
            squares = jnp.zeros((rows, 1), jnp.float32)
            for s in sources:
                wide = xg[i, s].astype(jnp.float32)
                squares += jnp.sum(wide * wide, axis=1, keepdims=True)
            return squares

        def normalize(sources, scale):
            for s in sources:
                wide = xg[i, s].astype(jnp.float32)
                normed[s] = (wide * gains[s, 0:1, :] * scale).astype(jnp.bfloat16)

        def product(sources, weight):
            total = None
            for s in sources:
                begin = pl.multiple_of(s * width, width)
                term = jnp.dot(normed[s], weight(pl.ds(begin, width)), preferred_element_type=jnp.float32)
                total = term if total is None else total + term
            return total

        def kv_rows(span):
            return wkv[slot, span, :]

        def query_rows(span):
            return wq[span, :]

        near_squares = total_squares(direct)
        near_scale = lax.rsqrt(near_squares / (2 * width) + EPS)
        normalize(direct, near_scale)
        near_kv = product(direct, kv_rows)
        near_query = product(direct, query_rows)
        for j in range(2):
            arrived(xg.at[i, passed_on[j]], fwd_recv.at[i, j])
        scale = lax.rsqrt((near_squares + total_squares(passed_on)) / (4 * width) + EPS)
        ratio = jnp.where(near_scale > 0.0, scale / near_scale, 0.0)
        normalize(passed_on, scale)
        raw_kv = near_kv * ratio + product(passed_on, kv_rows)
        pieces = []
        for j in range(2):
            turns_part = jnp.where(own_kv, 1.0 - j, key_part)
            kv_cos = cos * turns_part + (1.0 - turns_part)
            kv_sin = sin * turns_part
            piece = raw_kv[:, j * HD : (j + 1) * HD].astype(jnp.bfloat16).astype(jnp.float32)
            turned = piece * kv_cos + pltpu.roll(piece, HD // 2, 1) * kv_sin
            pieces.append(turned.astype(jnp.bfloat16))

        @pl.when(own_kv)
        def _():
            keys[pl.ds(start, rows), :] = pieces[0]
            values[pl.ds(start, rows), :] = pieces[1]

        @pl.when(jnp.logical_not(own_kv))
        def _():
            for j in range(2):
                kv_send_buf[i, j] = pieces[j]
            for j in range(2):
                target = kv_target(j)

                @pl.when(target != me)
                def _():
                    kv_remote(i, j, target).start()

                @pl.when(target == me)
                def _():
                    pltpu.make_async_copy(
                        kv_send_buf.at[i, j], kv_in.at[i, kind], kv_recv.at[i, kind]
                    ).start()

        raw_query = near_query * ratio + product(passed_on, query_rows)
        turned = []
        for h in range(local_heads):
            u = raw_query[:, h * HD : (h + 1) * HD]
            turned.append((u * cos + pltpu.roll(u, HD // 2, 1) * sin).astype(jnp.bfloat16))
        queries[i] = jnp.concatenate(turned, axis=0)

    def stage_attend(i):
        start = pl.multiple_of(i * rows, rows)
        visible = jnp.concatenate([seen[pl.ds(start, rows), :]] * local_heads, axis=0) > 0.5

        @pl.when(jnp.logical_not(moves_weights & (i >= first_moved)))
        def _():
            for k in range(2):
                arrived(kv_in.at[i, k], kv_recv.at[i, k])
            keys[pl.ds(start, rows), :] = kv_in[i, 0]
            values[pl.ds(start, rows), :] = kv_in[i, 1]

        scores = (
            lax.dot_general(
                queries[i], keys[...], (((1,), (1,)), ((), ())), preferred_element_type=jnp.float32
            )
            * scale_scores
        )
        scores = jnp.where(visible, scores, NEG)
        top = jnp.max(scores, axis=1, keepdims=True)
        weights = jnp.where(visible, jnp.exp(scores - top), 0.0)
        denom = jnp.sum(weights, axis=1, keepdims=True)
        mixed = jnp.dot(weights.astype(jnp.bfloat16), values[...], preferred_element_type=jnp.float32)
        mixed = (mixed / denom).astype(jnp.bfloat16)
        for h in range(local_heads):
            heads[i, me, :, h * HD : (h + 1) * HD] = mixed[h * rows : (h + 1) * rows, :]
        for j in (2, 1, 0):
            heads_copy(i, j).start()

    def stage_output(i):
        @pl.when(i == 0)
        def _():
            out_copy.wait()

        start = pl.multiple_of(i * rows, rows)
        total = xg[i, me].astype(jnp.float32)
        for j in (None, 0, 2, 1):
            source = me if j is None else others[j]
            if j is not None:
                arrived(heads.at[i, source], h_recv.at[i, j])
            begin = pl.multiple_of(source * head_width, head_width)
            total += jnp.dot(
                heads[i, source], wo[pl.ds(begin, head_width), :], preferred_element_type=jnp.float32
            )
        out[pl.ds(pl.multiple_of(i * rows, BLK), rows), :] = total.astype(jnp.bfloat16)

        @pl.when(jnp.logical_not(is_last))
        def _():
            for copy in reversed(x_copies(i)):
                copy.start()


    orders = [packed(stages) for stages in ORDERS]

    def step(k, state):
        word, counts = state[0], state[1:]
        for w in range(len(orders[0])):
            fresh = jnp.where(section == 0, orders[0][w], jnp.where(section == 1, orders[1][w], jnp.where(section == 2, orders[2][w], orders[3][w])))
            word = jnp.where(k == w * PACKED, fresh, word)
        code = lax.rem(word, 4)
        for stage, run in enumerate((stage_forward, stage_project, stage_attend, stage_output)):

            @pl.when(code == stage)
            def _():
                run(counts[stage])

        after = [count + (code == stage).astype(jnp.int32) for stage, count in enumerate(counts)]
        return (word // 4, *after)

    lax.fori_loop(0, 4 * n_slices, step, (jnp.int32(0),) * 5)

    for j in range(3):
        gain_copy(j).wait_send()

    @pl.when(moves_weights)
    def _():
        for j in range(2):
            target = kv_target(j)

            @pl.when(target != me)
            def _():
                weight_remote(j, target).wait_send()

    @pl.loop(0, n_slices)
    def _(i):
        @pl.when(is_first)
        def _():
            diagonal_tokens(i).wait_send()

        @pl.when(jnp.logical_not(is_last))
        def _():
            for copy in x_copies(i):
                copy.wait_send()

        for j in range(2):
            forward(i, j).wait_send()
            target = kv_target(j)

            @pl.when((target != me) & jnp.logical_not(moves_weights & (i >= first_moved)))
            def _():
                kv_remote(i, j, target).wait_send()

        for j in range(3):
            heads_copy(i, j).wait_send()


def tables(count):
    index = np.arange(HD // 2, dtype=np.float32)
    freq = np.power(np.float32(THETA), np.float32(-2.0) * index / np.float32(HD)).astype(np.float32)
    angle = np.arange(count, dtype=np.float32)[:, None] * freq[None, :]
    cosine, sine = np.cos(angle), np.sin(angle)
    return np.concatenate([cosine, cosine, -sine, sine], axis=1).astype(np.float32)


def relay(n_pipe, tokens, norm_gain, query_weight, kv_weight, out_weight, window_blocks):
    count, width = tokens.shape
    n = PIECES
    rows = count // n
    w_query, w_kv, w_out = query_weight[0], kv_weight[0], out_weight[0]
    head_width = w_query.shape[1]
    padded = -(-count // LANES) * LANES
    anywhere = pl.BlockSpec(memory_space=pl.ANY)
    dma = pltpu.SemaphoreType.DMA
    states = pl.pallas_call(
        functools.partial(relay_kernel, n_pipe, n),
        out_shape=pltpu.VMEM((count, width), jnp.bfloat16),
        in_specs=[pl.BlockSpec(memory_space=pltpu.SMEM)] + [anywhere] * 6,
        out_specs=pl.BlockSpec(memory_space=pltpu.VMEM),
        scratch_shapes=[
            pltpu.VMEM((count, 2 * HD), jnp.float32),
            pltpu.VMEM((1, width), jnp.bfloat16),
            pltpu.VMEM((n, rows * (head_width // HD), HD), jnp.bfloat16),
            pltpu.VMEM(w_query.shape, jnp.bfloat16),
            pltpu.VMEM((2,) + w_kv.shape, jnp.bfloat16),
            pltpu.VMEM(w_out.shape, jnp.bfloat16),
            pltpu.VMEM((4, 8, width), jnp.float32),
            pltpu.VMEM((count, padded), jnp.float32),
            pltpu.VMEM((n, 4, rows, width), jnp.bfloat16),
            pltpu.VMEM((4, rows, width), jnp.bfloat16),
            pltpu.VMEM((n, 2, rows, HD), jnp.bfloat16),
            pltpu.VMEM((n, 2, rows, HD), jnp.bfloat16),
            pltpu.VMEM((padded, HD), jnp.bfloat16),
            pltpu.VMEM((padded, HD), jnp.bfloat16),
            pltpu.VMEM((n, 4, rows, head_width), jnp.bfloat16),
            dma((5,)),
            dma((3,)),
            dma((3,)),
            dma((n, 2)),
            dma((n, 2)),
            dma((n, 2)),
            dma((n, 2)),
            dma((n, 2)),
            dma((n, 2)),
            dma((n, 3)),
            dma((n, 3)),
            dma((2,)),
            dma((2,)),
        ],
        compiler_params=pltpu.CompilerParams(
            collective_id=0, has_side_effects=True, vmem_limit_bytes=56 * 1024 * 1024
        ),
        name="relay",
    )(window_blocks.T, tokens, norm_gain, tables(count), w_query, w_kv, w_out)
    return states[None]


def fits_relay(tokens, query_weight, kv_weight, n_tensor):
    return (
        n_tensor == 4
        and tokens.shape[0] % (PIECES * BLK) == 0
        and kv_weight.shape[2] == 2 * HD
        and query_weight.shape[2] == HQ * HD // 4
        and HQ // KVH == HQ // 4
    )


def program(n_pipe, n_tensor, *args):
    if fits_relay(args[0], args[2], args[3], n_tensor):
        return relay(n_pipe, *args)
    return local(*args)


def solution(mesh):
    placed = (
        P("seq", "tensor"),
        P("pipe", "tensor"),
        P("pipe", None, "tensor"),
        P("pipe", None, "tensor"),
        P("pipe", None, "tensor"),
        P("seq", None),
    )
    part = functools.partial(program, mesh.shape["pipe"], mesh.shape["tensor"])
    return jax.shard_map(
        part, mesh=mesh, in_specs=placed, out_specs=P("pipe", "seq", "tensor"), check_vma=False
    )
```

```python
import functools
import math

import jax
import jax.numpy as jnp
import numpy as np
from jax import lax
from jax.experimental import pallas as pl
from jax.experimental.pallas import tpu as pltpu
from jax.sharding import PartitionSpec as P

D = 4096
HD = 128
HQ = 16
KVH = 4
SLICE = 48
SLICES = 4
BLK = 16


EPS = 1e-05
THETA = 500000.0
NEG = -1e30


def from_behind(value, axis, steps):
    count = lax.axis_size(axis)
    initial, last = (max(0, -steps), min(count, count - steps))
    return lax.ppermute(value, axis, [(source, source + steps) for source in range(initial, last)])


def rotate(u, positions):
    half = u.shape[-1] // 2
    index = jnp.arange(half).astype(jnp.float32)
    freq = jnp.power(jnp.float32(THETA), -2.0 * index / u.shape[-1])
    angle = positions[:, None] * freq[None, :]
    cosine = jnp.cos(angle)[:, None, :]
    sine = jnp.sin(angle)[:, None, :]
    first = u[..., :half]
    second = u[..., half:]
    return jnp.concatenate(
        [first * cosine - second * sine, second * cosine + first * sine], axis=-1
    )


def local(tokens, norm_gain, query_weight, kv_weight, out_weight, window_blocks):
    n_pipe = lax.axis_size("pipe")
    section = lax.axis_index("pipe")
    member = lax.axis_index("tensor")
    width = tokens.shape[1]
    total_tokens = tokens.shape[0]
    w_query = query_weight[0]
    w_kv = kv_weight[0]
    w_out = out_weight[0]
    gain = norm_gain[0]
    local_heads = w_query.shape[1] // HD
    group = HQ // KVH
    kv_head = member * local_heads // group
    nblocks = window_blocks.shape[0]
    block_ids = jnp.arange(nblocks, dtype=jnp.int32)
    listed = jnp.any(window_blocks[:, :, None] == block_ids[None, None, :], axis=1)
    key_pos = jnp.arange(total_tokens, dtype=jnp.int32)
    slice_blocks = SLICE // BLK
    ticks = SLICES + n_pipe - 1

    def project_rows(piece):
        return (
            jnp.dot(piece, w_query, preferred_element_type=jnp.float32),
            jnp.dot(piece, w_kv, preferred_element_type=jnp.float32),
        )

    def apply_out(piece):
        return jnp.dot(piece, w_out, preferred_element_type=jnp.float32)

    def tick(step, carry):
        incoming, key_cache, value_cache, states = carry
        index = step - section
        valid = (index >= 0) & (index < SLICES)
        slot = jnp.clip(index, 0, SLICES - 1)
        start = slot * SLICE
        fresh = lax.dynamic_slice_in_dim(tokens, start, SLICE, 0)
        current = jnp.where(section == 0, fresh, incoming)
        wide = current.astype(jnp.float32)
        squares = lax.psum(jnp.sum(wide * wide, axis=1), "tensor")
        scale = lax.rsqrt(squares / D + EPS)
        normed = (wide * gain.astype(jnp.float32)[None, :] * scale[:, None]).astype(jnp.bfloat16)
        raw_query, raw_kv = project_rows(lax.all_gather(normed, "tensor", axis=1, tiled=True))
        positions = (start + jnp.arange(SLICE, dtype=jnp.int32)).astype(jnp.float32)
        queries = rotate(raw_query.reshape(SLICE, local_heads, HD), positions).astype(jnp.bfloat16)
        pairs = lax.all_gather(raw_kv.astype(jnp.bfloat16), "tensor", axis=1, tiled=True)
        keys_new = lax.dynamic_slice_in_dim(pairs, kv_head * HD, HD, 1)
        values_new = lax.dynamic_slice_in_dim(pairs, (KVH + kv_head) * HD, HD, 1)
        keys_rot = rotate(keys_new.astype(jnp.float32)[:, None, :], positions)[:, 0, :].astype(
            jnp.bfloat16
        )
        keys_written = lax.dynamic_update_slice_in_dim(key_cache, keys_rot, start, 0)
        values_written = lax.dynamic_update_slice_in_dim(value_cache, values_new, start, 0)
        scores = jnp.einsum(
            "qhd,kd->hqk", queries, keys_written, preferred_element_type=jnp.float32
        ) / math.sqrt(HD)
        query_pos = start + jnp.arange(SLICE, dtype=jnp.int32)
        query_rows = lax.dynamic_slice_in_dim(listed, slot * slice_blocks, slice_blocks, 0)
        visible = jnp.repeat(jnp.repeat(query_rows, BLK, axis=0), BLK, axis=1)
        visible = visible & (key_pos[None, :] <= query_pos[:, None])
        scores = jnp.where(visible[None], scores, NEG)
        top = jnp.max(scores, axis=-1, keepdims=True)
        weights_soft = jnp.where(visible[None], jnp.exp(scores - top), 0.0)
        denom = jnp.sum(weights_soft, axis=-1)
        probs = weights_soft.astype(jnp.bfloat16)
        mixed = jnp.einsum("hqk,kd->qhd", probs, values_written, preferred_element_type=jnp.float32)
        mixed = mixed / jnp.transpose(denom)[:, :, None]
        heads = mixed.astype(jnp.bfloat16).reshape(SLICE, local_heads * HD)
        projected = apply_out(lax.all_gather(heads, "tensor", axis=1, tiled=True))
        result = (wide + projected).astype(jnp.bfloat16)
        states_written = lax.dynamic_update_slice_in_dim(states, result, start, 0)
        states = jnp.where(valid, states_written, states)
        key_cache = jnp.where(valid, keys_written, key_cache)
        value_cache = jnp.where(valid, values_written, value_cache)
        passed = from_behind(result, "pipe", 1)
        return (passed, key_cache, value_cache, states)

    initial_carry = (
        jnp.zeros((SLICE, width), jnp.bfloat16),
        jnp.zeros((total_tokens, HD), jnp.bfloat16),
        jnp.zeros((total_tokens, HD), jnp.bfloat16),
        jnp.zeros((total_tokens, width), jnp.bfloat16),
    )
    final_carry = lax.fori_loop(0, ticks, tick, initial_carry)
    return final_carry[3][None]


PIECES = 6
LANES = 128
MESH = pl.DeviceIdType.MESH
FORWARD, PROJECT, ATTEND, OUTPUT = range(4)
PACKED = 12
FIRST_MOVED = 2
MOVED_AFTER = 0


ORDERS = tuple(
    ["FPAO".index(stage) for stage in order]
    for order in (
        "FPFAPFOAPFFOAPOAPFOAPOAO",
        "FPFAPFOAPOFAPFOAPFOAPOAO",
        "FPAFPAOFPAOFPAOFPOAFPAOO",
        "FPAFPAOFPAOFPAOFPOFAPAOO",
    )
)


def packed(stages):
    words = []
    for begin in range(0, len(stages), PACKED):
        words.append(sum(stage * 4**k for k, stage in enumerate(stages[begin : begin + PACKED])))
    return words


def relay_kernel(
    n_pipe,
    n_slices,
    window,
    tokens,
    gain,
    table,
    w_query,
    w_kv,
    w_out,
    out,
    turns,
    gain_row,
    queries,
    wq,
    wkv,
    wo,
    gains,
    seen,
    xg,
    normed,
    kv_send_buf,
    kv_in,
    keys,
    values,
    heads,
    w_sem,
    gain_send,
    gain_recv,
    x_recv,
    x_send,
    fwd_send,
    fwd_recv,
    kv_send,
    kv_recv,
    h_send,
    h_recv,
    wkv_send,
    wkv_recv,
):
    section = lax.axis_index("pipe")
    me = lax.axis_index("tensor")
    sibling = me + 1 - 2 * lax.rem(me, 2)
    across = lax.rem(me + 2, 4)
    diagonal = lax.rem(sibling + 2, 4)
    others = (sibling, across, diagonal)
    rows = xg.shape[2]
    width = xg.shape[3]
    padded = keys.shape[0]
    local_heads = wq.shape[1] // HD
    head_width = wq.shape[1]
    scale_scores = 1.0 / math.sqrt(HD)
    is_last = section == n_pipe - 1
    is_first = section == 0
    kind = me // 2
    moves_weights = section >= FIRST_MOVED
    first_moved = jnp.where(section >= 2, 0, MOVED_AFTER)
    direct = (jnp.where(is_first, me, sibling), jnp.where(is_first, diagonal, across))
    passed_on = (jnp.where(is_first, sibling, me), jnp.where(is_first, across, diagonal))

    def remote(src, dst, send, recv, target, pipe=None):
        where = {"tensor": target} if pipe is None else {"pipe": pipe, "tensor": target}
        return pltpu.make_async_remote_copy(
            src_ref=src, dst_ref=dst, send_sem=send, recv_sem=recv, device_id=where, device_id_type=MESH
        )

    kv_copy = pltpu.make_async_copy(w_kv, wkv.at[0], w_sem.at[0])
    query_copy = pltpu.make_async_copy(w_query, wq, w_sem.at[1])
    out_copy = pltpu.make_async_copy(w_out, wo, w_sem.at[2])
    table_copy = pltpu.make_async_copy(table, turns, w_sem.at[3])
    gain_load = pltpu.make_async_copy(gain, gain_row, w_sem.at[4])

    barrier = pltpu.get_barrier_semaphore()
    for peer in others:
        pl.semaphore_signal(barrier, inc=1, device_id={"tensor": peer}, device_id_type=MESH)

    @pl.when(jnp.logical_not(is_first))
    def _():
        for peer in (sibling, across):
            pl.semaphore_signal(
                barrier, inc=1, device_id={"pipe": section - 1, "tensor": peer}, device_id_type=MESH
            )

    @pl.when(jnp.logical_not(is_last))
    def _():
        for peer in (sibling, across):
            pl.semaphore_signal(
                barrier, inc=1, device_id={"pipe": section + 1, "tensor": peer}, device_id_type=MESH
            )

    for copy in (gain_load, kv_copy, query_copy, table_copy, out_copy):
        copy.start()
    keys[...] = jnp.zeros_like(keys)
    values[...] = jnp.zeros_like(values)
    gain_load.wait()
    gains[me] = jnp.broadcast_to(gain_row[...].astype(jnp.float32), (8, width))
    expected = 7 - 2 * is_first.astype(jnp.int32) - 2 * is_last.astype(jnp.int32)
    pl.semaphore_wait(barrier, expected)

    def own_tokens(i):
        return pltpu.make_async_copy(
            tokens.at[pl.ds(i * rows, rows)], xg.at[i, me], x_recv.at[i, 0]
        )

    def diagonal_tokens(i):
        return remote(
            tokens.at[pl.ds(i * rows, rows)], xg.at[i, me], x_send.at[i, 1], x_recv.at[i, 1], diagonal
        )

    @pl.when(is_first)
    def _():
        for i in range(2):
            diagonal_tokens(i).start()
            own_tokens(i).start()

    def gain_copy(j):
        return remote(gains.at[me], gains.at[me], gain_send.at[j], gain_recv.at[j], others[j])

    for j in range(3):
        gain_copy(j).start()

    def x_copies(i):
        return (
            remote(out.at[pl.ds(pl.multiple_of(i * rows, BLK), rows)], xg.at[i, me], x_send.at[i, 0], x_recv.at[i, 0], sibling, section + 1),
            remote(out.at[pl.ds(pl.multiple_of(i * rows, BLK), rows)], xg.at[i, me], x_send.at[i, 1], x_recv.at[i, 1], across, section + 1),
        )

    def forward(i, j):
        source = direct[j]
        return remote(xg.at[i, source], xg.at[i, source], fwd_send.at[i, j], fwd_recv.at[i, j], sibling)

    def heads_copy(i, j):
        return remote(heads.at[i, me], heads.at[i, me], h_send.at[i, j], h_recv.at[i, j], others[j])

    def kv_target(j):
        return lax.rem(2 * me + j, 4)

    def kv_remote(i, j, target):
        return remote(
            kv_send_buf.at[i, j], kv_in.at[i, kind], kv_send.at[i, j], kv_recv.at[i, kind], target
        )

    def weight_remote(j, target):
        return remote(
            w_kv.at[:, j * HD : (j + 1) * HD],
            wkv.at[1, :, pl.ds(pl.multiple_of(kind * HD, HD), HD)],
            wkv_send.at[j],
            wkv_recv.at[kind],
            target,
        )

    @pl.when(moves_weights)
    def _():
        for j in range(2):
            target = kv_target(j)

            @pl.when(target != me)
            def _():
                weight_remote(j, target).start()

            @pl.when(target == me)
            def _():
                pltpu.make_async_copy(
                    w_kv.at[:, j * HD : (j + 1) * HD],
                    wkv.at[1, :, pl.ds(pl.multiple_of(kind * HD, HD), HD)],
                    wkv_recv.at[kind],
                ).start()

    def arrived(dst, sem):
        pltpu.make_async_copy(dst, dst, sem).wait()

    column = lax.broadcasted_iota(jnp.int32, (BLK, padded), 1)
    row = lax.broadcasted_iota(jnp.int32, (BLK, padded), 0)
    column_block = column // BLK
    for block in range(n_slices * rows // BLK):
        listed = column_block == window[0, block]
        for j in range(1, 4):
            listed = listed | (column_block == window[j, block])
        causal = (column <= row + block * BLK) & (column < n_slices * rows)
        seen[block * BLK : (block + 1) * BLK, :] = jnp.where(listed & causal, 1.0, 0.0)

    key_part = (me < 2).astype(jnp.float32)

    def stage_forward(i):
        for j in range(2):
            arrived(xg.at[i, direct[j]], x_recv.at[i, j])
            forward(i, j).start()

        @pl.when(is_first & (i + 2 < n_slices))
        def _():
            diagonal_tokens(i + 2).start()
            own_tokens(i + 2).start()

    def stage_project(i):
        @pl.when(i == 0)
        def _():
            for j in range(3):
                gain_copy(j).wait_recv()
            kv_copy.wait()
            table_copy.wait()
            query_copy.wait()

        @pl.when(moves_weights & (i == first_moved))
        def _():
            for c in range(2):
                block = wkv.at[1, :, c * HD : (c + 1) * HD]
                arrived(block, wkv_recv.at[c])

        own_kv = moves_weights & (i >= first_moved)
        slot = own_kv.astype(jnp.int32)
        start = pl.multiple_of(i * rows, rows)
        cos = turns[pl.ds(start, rows), 0:HD]
        sin = turns[pl.ds(start, rows), HD : 2 * HD]

        def total_squares(sources):
            squares = jnp.zeros((rows, 1), jnp.float32)
            for s in sources:
                wide = xg[i, s].astype(jnp.float32)
                squares += jnp.sum(wide * wide, axis=1, keepdims=True)
            return squares

        def normalize(sources, scale):
            for s in sources:
                wide = xg[i, s].astype(jnp.float32)
                normed[s] = (wide * gains[s, 0:1, :] * scale).astype(jnp.bfloat16)

        def product(sources, weight):
            total = None
            for s in sources:
                begin = pl.multiple_of(s * width, width)
                term = jnp.dot(normed[s], weight(pl.ds(begin, width)), preferred_element_type=jnp.float32)
                total = term if total is None else total + term
            return total

        def kv_rows(span):
            return wkv[slot, span, :]

        def query_rows(span):
            return wq[span, :]

        near_squares = total_squares(direct)
        near_scale = lax.rsqrt(near_squares / (2 * width) + EPS)
        normalize(direct, near_scale)
        near_query = product(direct, query_rows)
        near_kv = product(direct, kv_rows)
        for j in range(2):
            arrived(xg.at[i, passed_on[j]], fwd_recv.at[i, j])
        scale = lax.rsqrt((near_squares + total_squares(passed_on)) / (4 * width) + EPS)
        ratio = jnp.where(near_scale > 0.0, scale / near_scale, 0.0)
        normalize(passed_on, scale)
        raw_kv = near_kv * ratio + product(passed_on, kv_rows)
        pieces = []
        for j in range(2):
            turns_part = jnp.where(own_kv, 1.0 - j, key_part)
            kv_cos = cos * turns_part + (1.0 - turns_part)
            kv_sin = sin * turns_part
            piece = raw_kv[:, j * HD : (j + 1) * HD].astype(jnp.bfloat16).astype(jnp.float32)
            turned = piece * kv_cos + pltpu.roll(piece, HD // 2, 1) * kv_sin
            pieces.append(turned.astype(jnp.bfloat16))

        @pl.when(own_kv)
        def _():
            keys[pl.ds(start, rows), :] = pieces[0]
            values[pl.ds(start, rows), :] = pieces[1]

        @pl.when(jnp.logical_not(own_kv))
        def _():
            for j in range(2):
                kv_send_buf[i, j] = pieces[j]
            for j in range(2):
                target = kv_target(j)

                @pl.when(target != me)
                def _():
                    kv_remote(i, j, target).start()

                @pl.when(target == me)
                def _():
                    pltpu.make_async_copy(
                        kv_send_buf.at[i, j], kv_in.at[i, kind], kv_recv.at[i, kind]
                    ).start()

        raw_query = near_query * ratio + product(passed_on, query_rows)
        turned = []
        for h in range(local_heads):
            u = raw_query[:, h * HD : (h + 1) * HD]
            turned.append((u * cos + pltpu.roll(u, HD // 2, 1) * sin).astype(jnp.bfloat16))
        queries[i] = jnp.concatenate(turned, axis=0)

    def stage_attend(i):
        start = pl.multiple_of(i * rows, rows)
        visible = jnp.concatenate([seen[pl.ds(start, rows), :]] * local_heads, axis=0) > 0.5

        @pl.when(jnp.logical_not(moves_weights & (i >= first_moved)))
        def _():
            for k in range(2):
                arrived(kv_in.at[i, k], kv_recv.at[i, k])
            keys[pl.ds(start, rows), :] = kv_in[i, 0]
            values[pl.ds(start, rows), :] = kv_in[i, 1]

        scores = (
            lax.dot_general(
                queries[i], keys[...], (((1,), (1,)), ((), ())), preferred_element_type=jnp.float32
            )
            * scale_scores
        )
        scores = jnp.where(visible, scores, NEG)
        top = jnp.max(scores, axis=1, keepdims=True)
        weights = jnp.where(visible, jnp.exp(scores - top), 0.0)
        denom = jnp.sum(weights, axis=1, keepdims=True)
        mixed = jnp.dot(weights.astype(jnp.bfloat16), values[...], preferred_element_type=jnp.float32)
        mixed = (mixed / denom).astype(jnp.bfloat16)
        for h in range(local_heads):
            heads[i, me, :, h * HD : (h + 1) * HD] = mixed[h * rows : (h + 1) * rows, :]
        for j in (2, 1, 0):
            heads_copy(i, j).start()

    def stage_output(i):
        @pl.when(i == 0)
        def _():
            out_copy.wait()

        start = pl.multiple_of(i * rows, rows)
        total = xg[i, me].astype(jnp.float32)
        for j in (None, 0, 2, 1):
            source = me if j is None else others[j]
            if j is not None:
                arrived(heads.at[i, source], h_recv.at[i, j])
            begin = pl.multiple_of(source * head_width, head_width)
            total += jnp.dot(
                heads[i, source], wo[pl.ds(begin, head_width), :], preferred_element_type=jnp.float32
            )
        out[pl.ds(pl.multiple_of(i * rows, BLK), rows), :] = total.astype(jnp.bfloat16)

        @pl.when(jnp.logical_not(is_last))
        def _():
            for copy in reversed(x_copies(i)):
                copy.start()


    orders = [packed(stages) for stages in ORDERS]

    def step(k, state):
        word, counts = state[0], state[1:]
        for w in range(len(orders[0])):
            fresh = jnp.where(section == 0, orders[0][w], jnp.where(section == 1, orders[1][w], jnp.where(section == 2, orders[2][w], orders[3][w])))
            word = jnp.where(k == w * PACKED, fresh, word)
        code = lax.rem(word, 4)
        for stage, run in enumerate((stage_forward, stage_project, stage_attend, stage_output)):

            @pl.when(code == stage)
            def _():
                run(counts[stage])

        after = [count + (code == stage).astype(jnp.int32) for stage, count in enumerate(counts)]
        return (word // 4, *after)

    lax.fori_loop(0, 4 * n_slices, step, (jnp.int32(0),) * 5)

    for j in range(3):
        gain_copy(j).wait_send()

    @pl.when(moves_weights)
    def _():
        for j in range(2):
            target = kv_target(j)

            @pl.when(target != me)
            def _():
                weight_remote(j, target).wait_send()

    @pl.loop(0, n_slices)
    def _(i):
        @pl.when(is_first)
        def _():
            diagonal_tokens(i).wait_send()

        @pl.when(jnp.logical_not(is_last))
        def _():
            for copy in x_copies(i):
                copy.wait_send()

        for j in range(2):
            forward(i, j).wait_send()
            target = kv_target(j)

            @pl.when((target != me) & jnp.logical_not(moves_weights & (i >= first_moved)))
            def _():
                kv_remote(i, j, target).wait_send()

        for j in range(3):
            heads_copy(i, j).wait_send()


def tables(count):
    index = np.arange(HD // 2, dtype=np.float32)
    freq = np.power(np.float32(THETA), np.float32(-2.0) * index / np.float32(HD)).astype(np.float32)
    angle = np.arange(count, dtype=np.float32)[:, None] * freq[None, :]
    cosine, sine = np.cos(angle), np.sin(angle)
    return np.concatenate([cosine, cosine, -sine, sine], axis=1).astype(np.float32)


def relay(n_pipe, tokens, norm_gain, query_weight, kv_weight, out_weight, window_blocks):
    count, width = tokens.shape
    n = PIECES
    rows = count // n
    w_query, w_kv, w_out = query_weight[0], kv_weight[0], out_weight[0]
    head_width = w_query.shape[1]
    padded = -(-count // LANES) * LANES
    anywhere = pl.BlockSpec(memory_space=pl.ANY)
    dma = pltpu.SemaphoreType.DMA
    states = pl.pallas_call(
        functools.partial(relay_kernel, n_pipe, n),
        out_shape=pltpu.VMEM((count, width), jnp.bfloat16),
        in_specs=[pl.BlockSpec(memory_space=pltpu.SMEM)] + [anywhere] * 6,
        out_specs=pl.BlockSpec(memory_space=pltpu.VMEM),
        scratch_shapes=[
            pltpu.VMEM((count, 2 * HD), jnp.float32),
            pltpu.VMEM((1, width), jnp.bfloat16),
            pltpu.VMEM((n, rows * (head_width // HD), HD), jnp.bfloat16),
            pltpu.VMEM(w_query.shape, jnp.bfloat16),
            pltpu.VMEM((2,) + w_kv.shape, jnp.bfloat16),
            pltpu.VMEM(w_out.shape, jnp.bfloat16),
            pltpu.VMEM((4, 8, width), jnp.float32),
            pltpu.VMEM((count, padded), jnp.float32),
            pltpu.VMEM((n, 4, rows, width), jnp.bfloat16),
            pltpu.VMEM((4, rows, width), jnp.bfloat16),
            pltpu.VMEM((n, 2, rows, HD), jnp.bfloat16),
            pltpu.VMEM((n, 2, rows, HD), jnp.bfloat16),
            pltpu.VMEM((padded, HD), jnp.bfloat16),
            pltpu.VMEM((padded, HD), jnp.bfloat16),
            pltpu.VMEM((n, 4, rows, head_width), jnp.bfloat16),
            dma((5,)),
            dma((3,)),
            dma((3,)),
            dma((n, 2)),
            dma((n, 2)),
            dma((n, 2)),
            dma((n, 2)),
            dma((n, 2)),
            dma((n, 2)),
            dma((n, 3)),
            dma((n, 3)),
            dma((2,)),
            dma((2,)),
        ],
        compiler_params=pltpu.CompilerParams(
            collective_id=0, has_side_effects=True, vmem_limit_bytes=56 * 1024 * 1024
        ),
        name="relay",
    )(window_blocks.T, tokens, norm_gain, tables(count), w_query, w_kv, w_out)
    return states[None]


def fits_relay(tokens, query_weight, kv_weight, n_tensor):
    return (
        n_tensor == 4
        and tokens.shape[0] % (PIECES * BLK) == 0
        and kv_weight.shape[2] == 2 * HD
        and query_weight.shape[2] == HQ * HD // 4
        and HQ // KVH == HQ // 4
    )


def program(n_pipe, n_tensor, *args):
    if fits_relay(args[0], args[2], args[3], n_tensor):
        return relay(n_pipe, *args)
    return local(*args)


def solution(mesh):
    placed = (
        P("seq", "tensor"),
        P("pipe", "tensor"),
        P("pipe", None, "tensor"),
        P("pipe", None, "tensor"),
        P("pipe", None, "tensor"),
        P("seq", None),
    )
    part = functools.partial(program, mesh.shape["pipe"], mesh.shape["tensor"])
    return jax.shard_map(
        part, mesh=mesh, in_specs=placed, out_specs=P("pipe", "seq", "tensor"), check_vma=False
    )
```
